32 devices in a mesh: sub: 16 (over z, y, x), coarse: 2 (over core).
Axes of the slice: x: 2, y: 2, z: 4, core: 2. Of those that a mesh axis runs over, the one named last changes fastest.
Arguments:
- right_side: float32 [2, 256, 96], P('coarse', 'sub'), may hold values from -6 to 6
- blocks: float32 [2, 256, 6, 96, 96], P('coarse', 'sub')
- pattern: int32 [2, 256, 6], P('coarse', 'sub'), may hold values from 0 to 31, as said below
- send_rows: int32 [2, 64, 4], P('coarse', 'sub'), may hold values from 0 to 15, as said below
- inverse_blocks: float32 [2, 256, 96, 96], P('coarse', 'sub')
- margin_blocks: float32 [2, 256, 96, 96], P('coarse', 'sub')
- near_null: float32 [2, 256, 6, 96], P('coarse', 'sub'), may hold values from -0.625 to 0.625
- aggregate: int32 [2, 256], P('coarse', 'sub'), may hold values from 0 to 7
- coarse_inverse: float32 [16, 48, 48], P('sub')
Outputs:
- solution: float32 [2, 256, 96], P('coarse', 'sub')
- residual: float32 [2, 256, 96], P('coarse', 'sub')
The draws below stay inside these ranges and needn't reach their ends.
Inputs may be any that keep to these rules, and one draw needn't show every extreme that they name: `pattern`: slot 0 of every block row names the row itself; in every other slot the rows of one subdomain name distinct extended rows. `send_rows`: the 4 rows one subdomain sends in one round are distinct.
All inputs are finite; a program needn't handle non-finite values.
Results may differ from the reference program's by a relative error of at most 0.0003.
Values sent between devices are 32-bit elements; how exact they have to be, the bound alone decides.
No kernel may reach another device: no remote copies, remote signals or barrier semaphores. Data moves between devices by JAX's collectives and lax.ppermute only.
A program may use at most 64 MiB of HBM per device.

```python
import math
import jax
import jax.numpy as jnp
from jax import lax

B = 96
ROWS = 16
GHOST = 4
NZ = 6
ROUNDS = 4
MODES = 6
NAGG = 8
ITERS = 3
EXT = 32
CDIM = 48
N_SUB = 16
N_COARSE = 2


def distinct_order(key, lead, count, keep):
    scores = jax.random.randint(key, lead + (count,), 0, 2 ** 20) * count + jnp.arange(count, dtype=jnp.int32)
    return jnp.argsort(scores, axis=-1)[..., :keep].astype(jnp.int32)


def signed_sizes(key, shape):
    raw = jax.random.uniform(key, shape, minval=-1.0, maxval=1.0)
    return jnp.sign(raw) * (0.5 + 0.5 * jnp.abs(raw))


def mixing_blocks(key, lead, width):
    keys = jax.random.split(key, 4)
    freqs = distinct_order(keys[0], lead, width, width)
    places = distinct_order(keys[1], lead, width, width)
    phase = (2 * places[..., None, :] + 1) * freqs[..., :, None] % (4 * width)
    norms = jnp.where(freqs == 0, math.sqrt(1.0 / width), math.sqrt(2.0 / width))
    basis = norms[..., :, None] * jnp.cos(phase.astype(jnp.float32) * (math.pi / (2 * width)))
    left = signed_sizes(keys[2], lead + (width,))
    right = signed_sizes(keys[3], lead + (width,))
    return left[..., :, None] * basis * right[..., None, :]


def definite_blocks(key, lead, width, low, high, mix):
    first, second = jax.random.split(key)
    diagonal = jax.random.uniform(first, lead + (width,), minval=low, maxval=high)
    mixed = mixing_blocks(second, lead, width)
    sym = 0.5 * (mixed + jnp.swapaxes(mixed, -1, -2))
    eye = jnp.eye(width, dtype=jnp.float32)
    return diagonal[..., None] * eye + mix * sym


def draw_pattern(key, part):
    order = distinct_order(key, (N_COARSE, N_SUB, NZ - 1), EXT, ROWS)
    others = jnp.transpose(order, (0, 1, 3, 2))
    own = jnp.broadcast_to(jnp.arange(ROWS, dtype=jnp.int32).reshape(1, 1, ROWS, 1), (N_COARSE, N_SUB, ROWS, 1))
    return jnp.concatenate([own, others], axis=3).reshape(N_COARSE, N_SUB * ROWS, NZ).astype(jnp.int32)


def draw_send_rows(key, part):
    order = distinct_order(key, (N_COARSE, N_SUB, ROUNDS), ROWS, GHOST)
    return order.reshape(N_COARSE, N_SUB * ROUNDS, GHOST)


def draw_blocks(key, part):
    first, second, third = jax.random.split(key, 3)
    lead = (N_COARSE, N_SUB * ROWS, NZ)
    mixed = mixing_blocks(first, lead, B)
    sym = 0.5 * (mixed + jnp.swapaxes(mixed, -1, -2))
    noise = jax.random.uniform(second, lead + (B, B), minval=-1.0, maxval=1.0) / B
    level = jax.random.uniform(third, (N_COARSE, N_SUB * ROWS, 1, 1, 1), minval=1.0, maxval=2.0)
    slots = jnp.arange(NZ, dtype=jnp.int32).reshape(1, 1, NZ, 1, 1)
    eye = jnp.eye(B, dtype=jnp.float32)
    first_slot = level * eye + 0.3 * sym + 0.03 * noise
    other_slot = -0.025 * eye + 0.015 * mixed + 0.005 * noise
    return jnp.where(slots == 0, first_slot, other_slot)


def draw_inverse_blocks(key, part):
    return definite_blocks(key, (N_COARSE, N_SUB * ROWS), B, 0.5, 1.0, 0.3)


def draw_margin_blocks(key, part):
    return definite_blocks(key, (N_COARSE, N_SUB * ROUNDS * GHOST), B, 0.25, 0.5, 0.15)


def draw_coarse_inverse(key, part):
    return definite_blocks(key, (N_SUB,), CDIM, 0.1, 0.2, 0.06)


def plant(array, rng, low, high):
    shape = array.shape
    index_at = [jax.random.randint(jax.random.fold_in(rng, axis), (), 0, shape[axis]) for axis in range(len(shape))]
    array = array.at[tuple(index_at)].set(low)
    longest = shape.index(max(shape))
    index_at[longest] = (index_at[longest] + 1) % shape[longest]
    return array.at[tuple(index_at)].set(high)


def shard_levels(rng, shape, cuts, smallest, top_value):
    factor_of = 1.0
    for axis_at, shards_of in cuts:
        steps = jax.random.uniform(jax.random.fold_in(jax.random.fold_in(rng, 6), axis_at), (shards_of,), jnp.float32, smallest / len(cuts), top_value / len(cuts))
        factor_of = factor_of * jnp.repeat(jnp.exp(steps), shape[axis_at] // shards_of).reshape((-1,) + (1,) * (len(shape) - 1 - axis_at))
    return factor_of


def centred(rng, extent, deviation, most, cuts=(), kind=jnp.bfloat16):
    drawn = deviation * jax.random.normal(rng, extent, jnp.float32)
    if cuts:
        drawn = drawn * shard_levels(rng, extent, cuts, -0.22, 0.18)
    return jnp.clip(drawn, -most, most).astype(kind)


def setup_inputs(seed: int = 0) -> dict:
    key_of = jax.random.split(jax.random.key(seed), 10)
    right_side = centred(key_of[0], (N_COARSE, N_SUB * ROWS, B), 1.0, 6.0, ((0, 2), (1, 16)), jnp.float32)
    blocks = draw_blocks(jax.random.fold_in(key_of[9], 71), 0)
    pattern = draw_pattern(jax.random.fold_in(key_of[9], 71), 0)
    send_rows = draw_send_rows(jax.random.fold_in(key_of[9], 71), 0)
    inverse_blocks = draw_inverse_blocks(jax.random.fold_in(key_of[9], 71), 0)
    margin_blocks = draw_margin_blocks(jax.random.fold_in(key_of[9], 71), 0)
    near_null = centred(key_of[6], (N_COARSE, N_SUB * ROWS, MODES, B), B ** -0.5, 0.625, ((0, 2), (1, 16)), jnp.float32)
    aggregate = plant(jax.random.randint(key_of[7], (N_COARSE, N_SUB * ROWS), 0, NAGG), jax.random.fold_in(key_of[7], 1), 0, NAGG - 1).astype(jnp.int32)
    coarse_inverse = draw_coarse_inverse(jax.random.fold_in(key_of[9], 71), 0)
    return dict(right_side=right_side, blocks=blocks, pattern=pattern, send_rows=send_rows, inverse_blocks=inverse_blocks, margin_blocks=margin_blocks, near_null=near_null, aggregate=aggregate, coarse_inverse=coarse_inverse)


highest = lax.Precision.HIGHEST


def reference(right_side, blocks, pattern, send_rows, inverse_blocks, margin_blocks, near_null, aggregate, coarse_inverse):
    levels = N_SUB.bit_length() - 1
    bit_list = [turn * levels // ROUNDS for turn in range(ROUNDS)]
    partners = [jnp.arange(N_SUB, dtype=jnp.int32) ^ (1 << bit_pos) for bit_pos in bit_list]
    matrix = blocks.reshape(N_COARSE, N_SUB, ROWS, NZ, B, B)
    columns = pattern.reshape(N_COARSE, N_SUB, ROWS * NZ)
    senders = send_rows.reshape(N_COARSE, N_SUB, ROUNDS, GHOST)
    inverse = inverse_blocks.reshape(N_COARSE, N_SUB, ROWS, B, B)
    margin = margin_blocks.reshape(N_COARSE, N_SUB, ROUNDS, GHOST, B, B)
    null_modes = near_null.reshape(N_COARSE, N_SUB, ROWS, MODES, B)
    groups_of = aggregate.reshape(N_COARSE, N_SUB, ROWS)
    coarse_idx = jnp.arange(N_COARSE, dtype=jnp.int32)[:, None, None]
    sub_idx = jnp.arange(N_SUB, dtype=jnp.int32)[None, :, None]
    flat_base = (jnp.arange(N_COARSE * N_SUB, dtype=jnp.int32) * EXT)[:, None] + columns.reshape(N_COARSE * N_SUB, ROWS * NZ)

    def operate(field):
        rims = []
        for turn in range(ROUNDS):
            partner = partners[turn]
            their_rows = senders[:, partner, turn, :]
            rims.append(field[coarse_idx, partner[None, :, None], their_rows])
        extended = jnp.concatenate([field] + rims, axis=2)
        picked = extended[coarse_idx, sub_idx, columns].reshape(N_COARSE, N_SUB, ROWS, NZ, B)
        forward = jnp.einsum("csrkab,csrkb->csra", matrix, picked, precision=highest)
        transposed = jnp.einsum("csrkab,csra->csrkb", matrix, field, precision=highest)
        spread = jnp.zeros((N_COARSE * N_SUB * EXT, B), field.dtype)
        spread = spread.at[flat_base.reshape(-1)].add(transposed.reshape(-1, B)).reshape(N_COARSE, N_SUB, EXT, B)
        back = spread[:, :, :ROWS]
        for turn in range(ROUNDS):
            partner = partners[turn]
            start = ROWS + turn * GHOST
            arrived = spread[:, partner, start:start + GHOST]
            back = back.at[coarse_idx, sub_idx, senders[:, :, turn, :]].add(arrived)
        return 0.5 * (forward + back)

    def precondition(residual):
        result = jnp.einsum("csrab,csrb->csra", inverse, residual, precision=highest)
        for turn in range(ROUNDS):
            partner = partners[turn]
            rows_here = senders[:, :, turn, :]
            values = residual[coarse_idx, sub_idx, rows_here]
            their_blocks = margin[:, partner, turn]
            result = result.at[coarse_idx, sub_idx, rows_here].add(jnp.einsum("csgab,csgb->csga", their_blocks, values, precision=highest))
        local = jnp.einsum("csrmb,csrb->csrm", null_modes, residual, precision=highest)
        table = (groups_of[..., None] == jnp.arange(NAGG, dtype=jnp.int32)).astype(residual.dtype)
        total = jnp.einsum("csrn,csrm->snm", table, local, precision=highest)
        solved = jnp.einsum("sij,sj->si", coarse_inverse, total.reshape(N_SUB, CDIM), precision=highest).reshape(N_SUB, NAGG, MODES)
        per_row = jnp.einsum("csrn,snm->csrm", table, solved, precision=highest)
        return result + jnp.einsum("csrmb,csrm->csrb", null_modes, per_row, precision=highest)

    source = right_side.reshape(N_COARSE, N_SUB, ROWS, B)
    solution = jnp.zeros_like(source)
    residual = source
    precond = precondition(residual)
    direction = precond
    product_now = jnp.sum(residual * precond)
    for step in range(ITERS):
        image = operate(direction)
        alpha = product_now / jnp.sum(direction * image)
        solution = solution + alpha * direction
        residual = residual - alpha * image
        if step + 1 < ITERS:
            precond = precondition(residual)
            product_next = jnp.sum(residual * precond)
            direction = precond + (product_next / product_now) * direction
            product_now = product_next
    return solution.reshape(N_COARSE, N_SUB * ROWS, B), residual.reshape(N_COARSE, N_SUB * ROWS, B)
```

```python
import functools

import jax
import jax.numpy as jnp
from jax import lax
from jax.experimental import pallas as pl
from jax.experimental.pallas import tpu as pltpu
from jax.sharding import PartitionSpec as P

ITERS = 3
SHIFT = 2.0

f32 = jnp.float32
VMEM = pl.BlockSpec(memory_space=pltpu.VMEM)
SMEM = pl.BlockSpec(memory_space=pltpu.SMEM)


def partner(array, axis, bit):
    return lax.ppermute(array, axis, [(i, i ^ 1 << bit) for i in range(lax.axis_size(axis))])


def call(kernel, outs, in_specs, args, scratch=(), name=None, flops=1000000):
    return pl.pallas_call(
        kernel,
        out_shape=[jax.ShapeDtypeStruct(shape, f32) for shape in outs],
        in_specs=in_specs,
        out_specs=[VMEM] * len(outs),
        scratch_shapes=list(scratch),
        compiler_params=pltpu.CompilerParams(vmem_limit_bytes=12 * 1024 * 1024),
        cost_estimate=pl.CostEstimate(flops=flops, bytes_accessed=100000, transcendentals=0),
        name=name,
    )(*args)


def eye_mask(width):
    return lax.broadcasted_iota(jnp.int32, (width, width), 0) == lax.broadcasted_iota(
        jnp.int32, (width, width), 1
    )


def to_column(row, eye):
    return jnp.sum(jnp.where(eye, row, 0.0), axis=1, keepdims=True)


def to_row(column, eye):
    return jnp.sum(jnp.where(eye, column, 0.0), axis=0, keepdims=True)


def restrict(null_ref, aggregate_ref, field, rows, modes):
    lane = lax.broadcasted_iota(jnp.int32, (modes, 128), 1)
    mode = lax.broadcasted_iota(jnp.int32, (modes, 128), 0)
    shifted = lane - mode
    total = jnp.zeros((modes, 128), f32)
    for i in range(rows):
        dots = jnp.sum(null_ref[0, i] * field[i : i + 1], axis=1, keepdims=True)
        total = total + jnp.where(shifted == aggregate_ref[0, i] * modes, dots, 0.0)
    return jnp.sum(total, axis=0, keepdims=True)


def pack_kernel(margin_ref, *outs):
    turns = len(outs)
    ghosts = margin_ref.shape[1] // turns
    width = margin_ref.shape[2]
    tall = width * width // 128
    side = 128 - width
    rest = width - tall
    for turn in range(turns):
        for g in range(ghosts):
            block = margin_ref[0, turn * ghosts + g]
            outs[turn][g, :, 0:width] = block[:tall]
            for piece in range(width // side):
                outs[turn][g, piece * rest : (piece + 1) * rest, width:128] = block[
                    tall:, piece * side : (piece + 1) * side
                ]


def restrict_kernel(field_ref, null_ref, aggregate_ref, out_ref):
    rows = field_ref.shape[1]
    out_ref[...] = restrict(null_ref, aggregate_ref, field_ref[0], rows, null_ref.shape[2])


def local_kernel(field_ref, inverse_ref, column_ref, row_ref):
    rows, width = field_ref.shape
    eye = eye_mask(width)
    for i in range(rows):
        column = jnp.sum(inverse_ref[i] * field_ref[i : i + 1, :], axis=1, keepdims=True)
        column_ref[i] = jnp.broadcast_to(column, (width, 128))
        row_ref[i : i + 1, :] = to_row(column, eye)


def coarse_rows(mine_ref, theirs_ref, solver_ref, null_ref, aggregate_ref, spots_ref):
    size = solver_ref.shape[1]
    rows, modes, width = null_ref.shape[1:]
    total = mine_ref[...] + theirs_ref[...]
    solved = jnp.sum(solver_ref[0] * total[:, :size], axis=1, keepdims=True)
    for a in range(size // modes):
        spots_ref[a] = jnp.broadcast_to(solved[a * modes : (a + 1) * modes], (modes, width))
    return [
        jnp.sum(spots_ref[aggregate_ref[0, i]] * null_ref[0, i], axis=0, keepdims=True)
        for i in range(rows)
    ]


def spread_block_row(blocks_ref, pattern_ref, slots_ref, i, column):
    for j in range(blocks_ref.shape[2]):
        slots_ref[j, pl.ds(pattern_ref[0, i, j], 1), :] = jnp.sum(
            blocks_ref[0, i, j] * column, axis=0, keepdims=True
        )


def finish_spread(slots_ref, senders_ref, z_ref, own_ref, packets, rows):
    turns = len(packets)
    ghosts = senders_ref.shape[2]
    spread = slots_ref[0]
    for j in range(1, slots_ref.shape[0]):
        spread = spread + slots_ref[j]
    own_ref[...] = spread[:rows]
    for turn in range(turns):
        start = rows + turn * ghosts
        for g in range(ghosts):
            packets[turn][g : g + 1, :] = z_ref[pl.ds(senders_ref[0, turn, g], 1), :]
        packets[turn][ghosts:, :] = spread[start : start + ghosts]


def first_kernel(
    turns,
    field_ref,
    inverse_ref,
    *refs,
):
    gathered = refs[:turns]
    (
        mine_ref,
        theirs_ref,
        solver_ref,
        null_ref,
        blocks_ref,
        aggregate_ref,
        pattern_ref,
        senders_ref,
        combined_ref,
        z_ref,
        own_ref,
    ) = refs[turns : turns + 11]
    packets = refs[turns + 11 : 2 * turns + 11]
    spots_ref, slots_ref = refs[2 * turns + 11 :]
    rows, width = z_ref.shape
    tall = width * width // 128
    side = 128 - width
    rest = width - tall
    ghosts = senders_ref.shape[2]
    eye = eye_mask(width)
    combined_ref[...] = inverse_ref[0]
    for turn in range(turns):
        for g in range(ghosts):
            at = senders_ref[0, turn, g]
            combined_ref[at, 0:tall, :] += gathered[turn][g, :, 0:width]
            for piece in range(width // side):
                combined_ref[at, tall:, piece * side : (piece + 1) * side] += gathered[turn][
                    g, piece * rest : (piece + 1) * rest, width:128
                ]
    slots_ref[...] = jnp.zeros(slots_ref.shape, f32)
    coarse = coarse_rows(mine_ref, theirs_ref, solver_ref, null_ref, aggregate_ref, spots_ref)
    for i in range(rows):
        product = combined_ref[i] * field_ref[0, i : i + 1, :] + jnp.where(eye, coarse[i], 0.0)
        column = jnp.sum(product, axis=1, keepdims=True)
        z_ref[i : i + 1, :] = to_row(column, eye)
        spread_block_row(blocks_ref, pattern_ref, slots_ref, i, column)
    finish_spread(slots_ref, senders_ref, z_ref, own_ref, packets, rows)


def spread_kernel(
    turns,
    column_ref,
    row_ref,
    mine_ref,
    theirs_ref,
    solver_ref,
    null_ref,
    blocks_ref,
    aggregate_ref,
    pattern_ref,
    senders_ref,
    z_ref,
    own_ref,
    *refs,
):
    packets = refs[:turns]
    spots_ref, slots_ref = refs[turns:]
    rows, width = z_ref.shape
    eye = eye_mask(width)
    slots_ref[...] = jnp.zeros(slots_ref.shape, f32)
    coarse = coarse_rows(mine_ref, theirs_ref, solver_ref, null_ref, aggregate_ref, spots_ref)
    for i in range(rows):
        z_ref[i : i + 1, :] = row_ref[i : i + 1, :] + coarse[i]
        column = column_ref[i][:, :width] + to_column(coarse[i], eye)
        spread_block_row(blocks_ref, pattern_ref, slots_ref, i, column)
    finish_spread(slots_ref, senders_ref, z_ref, own_ref, packets, rows)


def apply_rows(turns, arrived, z_ref, own_ref, blocks_ref, pattern_ref, senders_ref, extended_ref, back_ref):
    rows, width = z_ref.shape
    ghosts = senders_ref.shape[2]
    eye = eye_mask(width)
    extended_ref[0:rows, :] = z_ref[...]
    back_ref[...] = jnp.zeros(back_ref.shape, f32)
    for turn in range(turns):
        start = rows + turn * ghosts
        extended_ref[start : start + ghosts, :] = arrived[turn][0:ghosts, :]
        for g in range(ghosts):
            back_ref[turn, pl.ds(senders_ref[0, turn, g], 1), :] = arrived[turn][
                ghosts + g : ghosts + g + 1, :
            ]
    back = own_ref[...]
    for turn in range(turns):
        back = back + back_ref[turn]
    image = []
    for i in range(rows):
        total = blocks_ref[0, i, 0] * extended_ref[i : i + 1, :]
        for j in range(1, blocks_ref.shape[2]):
            total = total + blocks_ref[0, i, j] * extended_ref[pl.ds(pattern_ref[0, i, j], 1), :]
        column = jnp.sum(total, axis=1, keepdims=True)
        image.append(to_row(column, eye))
    return 0.5 * (jnp.concatenate(image, axis=0) + back)


def apply_kernel(turns, field_ref, z_ref, own_ref, *refs):
    arrived = refs[:turns]
    (
        blocks_ref,
        null_ref,
        pattern_ref,
        senders_ref,
        aggregate_ref,
        next_ref,
        coarse_ref,
        extended_ref,
        back_ref,
    ) = refs[turns:]
    image = apply_rows(
        turns, arrived, z_ref, own_ref, blocks_ref, pattern_ref, senders_ref, extended_ref, back_ref
    )
    following = image - SHIFT * field_ref[...].reshape(image.shape)
    next_ref[...] = following
    rows = image.shape[0]
    coarse_ref[...] = restrict(null_ref, aggregate_ref, following, rows, null_ref.shape[2])


def last_kernel(turns, fields, *refs):
    field_refs = refs[:fields]
    z_refs = refs[fields : 2 * fields]
    own_ref = refs[2 * fields]
    arrived = refs[2 * fields + 1 : 2 * fields + 1 + turns]
    blocks_ref, pattern_ref, senders_ref, next_ref, dots_ref, extended_ref, back_ref = refs[
        2 * fields + 1 + turns :
    ]
    image = apply_rows(
        turns,
        arrived,
        z_refs[-1],
        own_ref,
        blocks_ref,
        pattern_ref,
        senders_ref,
        extended_ref,
        back_ref,
    )
    following = image - SHIFT * field_refs[-1][...]
    next_ref[...] = following
    lane = lax.broadcasted_iota(jnp.int32, (1, 128), 1)
    values = [ref[...].reshape(image.shape) for ref in field_refs] + [following]
    packed = jnp.zeros((1, 128), f32)
    for a, value in enumerate(values):
        for c, z_at in enumerate(z_refs):
            column = jnp.sum(value * z_at[...], axis=0, keepdims=True)
            dot = jnp.sum(column, axis=1, keepdims=True)
            packed = jnp.where(lane == a * fields + c, dot, packed)
    dots_ref[...] = jnp.broadcast_to(packed.reshape(1, 1, 128), dots_ref.shape)


def finish_kernel(fields, dots_ref, *refs):
    value_refs = refs[: fields + 1]
    z_refs = refs[fields + 1 : 2 * fields + 1]
    solution_ref, residual_ref = refs[2 * fields + 1 :]
    total = jnp.sum(dots_ref[...], axis=0)
    lane = lax.broadcasted_iota(jnp.int32, (1, 128), 1)
    shape = solution_ref.shape[1:]
    gram = [
        [
            jnp.sum(jnp.where(lane == a * fields + c, total, 0.0), axis=1, keepdims=True)
            for c in range(fields)
        ]
        for a in range(fields + 1)
    ]
    zero = jnp.zeros((1, 1), f32)
    one = jnp.ones((1, 1), f32)

    def form(left, right):
        value = zero
        for a, left_at in enumerate(left):
            if left_at is None:
                continue
            for c, right_at in enumerate(right):
                if right_at is not None:
                    value = value + left_at * right_at * gram[a][c]
        return value

    def plus(first, second):
        if first is None:
            return second
        return first if second is None else first + second

    def scaled(scale, value):
        return None if value is None else scale * value

    residual = [one] + [None] * fields
    direction = [one] + [None] * (fields - 1)
    iterate = [None] * fields
    product_now = form(residual, direction)
    for step in range(fields):
        image = [None] * (fields + 1)
        for c in range(fields):
            if direction[c] is not None:
                image[c] = plus(image[c], SHIFT * direction[c])
                image[c + 1] = plus(image[c + 1], direction[c])
        alpha = product_now / form(image, direction)
        iterate = [plus(iterate[c], scaled(alpha, direction[c])) for c in range(fields)]
        residual = [plus(residual[a], scaled(-alpha, image[a])) for a in range(fields + 1)]
        if step + 1 < fields:
            product_next = form(residual, residual[:fields])
            beta = product_next / product_now
            direction = [plus(residual[c], scaled(beta, direction[c])) for c in range(fields)]
            product_now = product_next
    answer = iterate[0] * z_refs[0][...]
    for c in range(1, fields):
        answer = answer + iterate[c] * z_refs[c][...]
    left_over = residual[0] * value_refs[0][...].reshape(shape)
    for a in range(1, fields + 1):
        left_over = left_over + residual[a] * value_refs[a][...]
    solution_ref[0] = answer
    residual_ref[0] = left_over


def on_device(
    right_side,
    blocks,
    pattern,
    send_rows,
    inverse_blocks,
    margin_blocks,
    near_null,
    aggregate,
    coarse_inverse,
):
    rows, width = right_side.shape[1:]
    slots = blocks.shape[2]
    turns, ghosts = send_rows.shape[1:]
    extent = rows + turns * ghosts
    modes = near_null.shape[2]
    groups = coarse_inverse.shape[1] // modes
    levels = lax.axis_size("sub").bit_length() - 1
    bits = [turn * levels // turns for turn in range(turns)]
    devices = lax.axis_size("sub") * lax.axis_size("coarse")
    flip = [(0, 1), (1, 0)]
    row_shape = (rows, width)
    packet = (2 * ghosts, width)
    slot_scratch = [
        pltpu.VMEM((groups, modes, width), f32),
        pltpu.VMEM((slots, extent, width), f32),
    ]
    apply_scratch = [pltpu.VMEM((extent, width), f32), pltpu.VMEM((turns, rows, width), f32)]

    def swap(array):
        return lax.ppermute(array, "coarse", flip)

    packs = call(
        pack_kernel,
        [(ghosts, width * width // 128, 128)] * turns,
        [VMEM],
        [margin_blocks],
        name="pack_margin",
    )
    gathered = [partner(packs[turn], "sub", bits[turn]) for turn in range(turns)]
    (mine,) = call(
        restrict_kernel,
        [(1, 128)],
        [VMEM, VMEM, SMEM],
        [right_side, near_null, aggregate],
        name="restrict",
    )
    theirs = swap(mine)
    combined, z, own, *packets = call(
        functools.partial(first_kernel, turns),
        [(rows, width, width), row_shape, row_shape] + [packet] * turns,
        [VMEM] * (turns + 7) + [SMEM] * 3,
        [right_side, inverse_blocks, *gathered, mine, theirs, coarse_inverse, near_null, blocks]
        + [aggregate, pattern, send_rows],
        scratch=slot_scratch,
        name="first_spread",
    )
    values = [right_side]
    fields = [z]
    for step in range(ITERS):
        arrived = [partner(packets[turn], "sub", bits[turn]) for turn in range(turns)]
        if step + 1 == ITERS:
            break
        following, mine = call(
            functools.partial(apply_kernel, turns),
            [row_shape, (1, 128)],
            [VMEM] * (turns + 5) + [SMEM] * 3,
            [values[-1], fields[-1], own, *arrived, blocks, near_null, pattern, send_rows, aggregate],
            scratch=apply_scratch,
            name="apply",
        )
        values.append(following)
        theirs = swap(mine)
        column, row = call(
            local_kernel,
            [(rows, width, 128), row_shape],
            [VMEM, VMEM],
            [following, combined],
            name="local_inverse",
        )
        z, own, *packets = call(
            functools.partial(spread_kernel, turns),
            [row_shape, row_shape] + [packet] * turns,
            [VMEM] * 7 + [SMEM] * 3,
            [column, row, mine, theirs, coarse_inverse, near_null, blocks]
            + [aggregate, pattern, send_rows],
            scratch=slot_scratch,
            name="spread",
        )
        fields.append(z)
    following, dots = call(
        functools.partial(last_kernel, turns, ITERS),
        [row_shape, (devices, 1, 128)],
        [VMEM] * (2 * ITERS + 1 + turns + 1) + [SMEM] * 2,
        [*values, *fields, own, *arrived, blocks, pattern, send_rows],
        scratch=apply_scratch,
        name="last_apply",
    )
    values.append(following)
    exchanged = lax.all_to_all(dots, ("sub", "coarse"), 0, 0)
    answer, left_over = call(
        functools.partial(finish_kernel, ITERS),
        [right_side.shape] * 2,
        [VMEM] * (2 * ITERS + 2),
        [exchanged, *values, *fields],
        name="finish",
    )
    return answer, left_over


def solution(mesh):
    in_specs = (
        P("coarse", "sub", None),
        P("coarse", "sub", None, None, None),
        P("coarse", "sub", None),
        P("coarse", "sub", None),
        P("coarse", "sub", None, None),
        P("coarse", "sub", None, None),
        P("coarse", "sub", None, None),
        P("coarse", "sub"),
        P("sub", None, None),
    )
    out_specs = (P("coarse", "sub", None), P("coarse", "sub", None))
    return jax.shard_map(
        on_device, mesh=mesh, in_specs=in_specs, out_specs=out_specs, check_vma=False
    )
```

```python
import functools

import jax
import jax.numpy as jnp
from jax import lax
from jax.experimental import pallas as pl
from jax.experimental.pallas import tpu as pltpu
from jax.sharding import PartitionSpec as P

ITERS = 3
SHIFT = 2.0
REPEATS = 16

f32 = jnp.float32
bf16 = jnp.bfloat16
VMEM = pl.BlockSpec(memory_space=pltpu.VMEM)
ANY = pl.BlockSpec(memory_space=pl.ANY)
SMEM = pl.BlockSpec(memory_space=pltpu.SMEM)


def partner(array, axis, bit):
    return lax.ppermute(array, axis, [(i, i ^ 1 << bit) for i in range(lax.axis_size(axis))])


def call(kernel, outs, in_specs, args, scratch=(), name=None, cost=100000):
    return pl.pallas_call(
        kernel,
        out_shape=[
            jax.ShapeDtypeStruct(*(out if isinstance(out[0], tuple) else (out, f32))) for out in outs
        ],
        in_specs=in_specs,
        out_specs=[VMEM] * len(outs),
        scratch_shapes=list(scratch),
        compiler_params=pltpu.CompilerParams(vmem_limit_bytes=12 * 1024 * 1024),
        cost_estimate=pl.CostEstimate(flops=0, bytes_accessed=cost, transcendentals=0),
        name=name,
    )(*args)


def eye_mask(width):
    return lax.broadcasted_iota(jnp.int32, (width, width), 0) == lax.broadcasted_iota(
        jnp.int32, (width, width), 1
    )


def to_column(row, eye):
    return jnp.sum(jnp.where(eye, row, 0.0), axis=1, keepdims=True)


def to_row(column, eye):
    return jnp.sum(jnp.where(eye, column, 0.0), axis=0, keepdims=True)


def restrict(null_ref, offset_ref, field):
    offset = offset_ref[...]
    total = jnp.zeros(offset.shape, f32)
    for mode in range(null_ref.shape[1]):
        dots = jnp.sum(null_ref[0, mode] * field, axis=1, keepdims=True)
        total = total + jnp.where(offset == mode, dots, 0.0)
    return jnp.sum(total, axis=0, keepdims=True)


def coarse_field(mine_ref, theirs_ref, solver_ref, null_ref, offset_ref):
    size = solver_ref.shape[1]
    total = mine_ref[...] + theirs_ref[...]
    solved = jnp.sum(solver_ref[0] * total[:, :size], axis=1, keepdims=True)
    flat = to_row(solved, eye_mask(size))
    offset = offset_ref[:, :size]
    field = None
    for mode in range(null_ref.shape[1]):
        weight = jnp.sum(jnp.where(offset == mode, flat, 0.0), axis=1, keepdims=True)
        term = null_ref[0, mode] * weight
        field = term if field is None else field + term
    return field


def thirds(value):
    high = value.astype(bf16)
    rest = value - high.astype(f32)
    middle = rest.astype(bf16)
    low = (rest - middle.astype(f32)).astype(bf16)
    return jnp.concatenate([high, middle, low], axis=0)


def select_rows(table_ref, value):
    return jnp.dot(table_ref[...], thirds(value), preferred_element_type=f32)


def triple(table):
    return jnp.concatenate([table.astype(bf16)] * 3, axis=1)


def pack_kernel(margin_ref, *refs):
    outs = refs[REPEATS:]
    turns = len(outs)
    ghosts = margin_ref.shape[1] // turns
    width = margin_ref.shape[2]
    tall = width * width // 128
    side = 128 - width
    rest = width - tall
    for turn in range(turns):
        for g in range(ghosts):
            block = margin_ref[0, turn * ghosts + g]
            outs[turn][g, :, 0:width] = block[:tall]
            for piece in range(width // side):
                outs[turn][g, piece * rest : (piece + 1) * rest, width:128] = block[
                    tall:, piece * side : (piece + 1) * side
                ]


def restrict_kernel(field_ref, null_ref, aggregate_ref, offset_ref, mine_ref):
    modes = null_ref.shape[1]
    lane = lax.broadcasted_iota(jnp.int32, (1, 128), 1)
    for i in range(offset_ref.shape[0]):
        offset_ref[i : i + 1, :] = lane - aggregate_ref[0, i] * modes
    mine_ref[...] = restrict(null_ref, offset_ref, field_ref[0])


def table_kernel(
    pattern_ref, senders_ref, pick_ref, spread_ref, send_ref, back_ref, table_ref, send_table_ref
):
    slots, _, rows = pattern_ref.shape
    turns, ghosts = senders_ref.shape[1:]
    extent = pick_ref.shape[1] // 3
    lane = lax.broadcasted_iota(jnp.int32, (1, 128), 1)
    for i in range(rows):
        for j in range(slots):
            at = i * slots + j
            table_ref[at : at + 1, :] = jnp.where(lane == pattern_ref[j, 0, i], 1.0, 0.0)
    for turn in range(turns):
        for g in range(ghosts):
            at = turn * ghosts + g
            send_table_ref[at : at + 1, :] = jnp.where(lane == senders_ref[0, turn, g], 1.0, 0.0)
    table = table_ref[...]
    pick_ref[...] = triple(table[:, :extent])
    spread_ref[...] = triple(table.T[:extent])
    send_table = send_table_ref[...]
    send_ref[...] = triple(send_table[:, :rows])
    back_ref[...] = triple(send_table.T[:rows])


def local_kernel(field_ref, inverse_ref, column_ref, row_ref):
    rows, width = field_ref.shape
    eye = eye_mask(width)
    for i in range(rows):
        column = jnp.sum(inverse_ref[i] * field_ref[i : i + 1, :], axis=1, keepdims=True)
        column_ref[i] = jnp.broadcast_to(column, (width, 128))
        row_ref[i : i + 1, :] = to_row(column, eye)


def spread_block_row(blocks_ref, parts_ref, i, column):
    slots = blocks_ref.shape[2]
    for j in range(slots):
        at = i * slots + j
        parts_ref[at : at + 1, :] = jnp.sum(blocks_ref[0, i, j] * column, axis=0, keepdims=True)


def finish_spread(parts_ref, spread_ref, send_ref, z, own_ref, packets):
    turns = len(packets)
    rows = z.shape[0]
    sent = select_rows(send_ref, z)
    spread = select_rows(spread_ref, parts_ref[...])
    own_ref[...] = spread[:rows]
    ghosts = sent.shape[0] // turns
    for turn in range(turns):
        start = turn * ghosts
        packets[turn][0:ghosts, :] = sent[start : start + ghosts]
        packets[turn][ghosts:, :] = spread[rows + start : rows + start + ghosts]


def first_kernel(turns, field_ref, inverse_ref, *refs):
    gathered = refs[:turns][::-1]
    (
        mine_ref,
        theirs_ref,
        solver_ref,
        null_ref,
        offset_ref,
        blocks_ref,
        spread_ref,
        send_ref,
        senders_ref,
        combined_ref,
        z_ref,
        own_ref,
    ) = refs[turns : turns + 12]
    packets = refs[turns + 12 : 2 * turns + 12]
    (parts_ref,) = refs[2 * turns + 12 :]
    rows, width = z_ref.shape
    tall = width * width // 128
    side = 128 - width
    rest = width - tall
    ghosts = senders_ref.shape[2]
    eye = eye_mask(width)
    combined_ref[...] = inverse_ref[0]
    for turn in range(turns):
        for g in range(ghosts):
            at = senders_ref[0, turn, g]
            combined_ref[at, 0:tall, :] += gathered[turn][g, :, 0:width]
            for piece in range(width // side):
                combined_ref[at, tall:, piece * side : (piece + 1) * side] += gathered[turn][
                    g, piece * rest : (piece + 1) * rest, width:128
                ]
    coarse = coarse_field(mine_ref, theirs_ref, solver_ref, null_ref, offset_ref)
    for i in range(rows):
        product = combined_ref[i] * field_ref[0, i : i + 1, :] + jnp.where(eye, coarse[i : i + 1], 0.0)
        column = jnp.sum(product, axis=1, keepdims=True)
        z_ref[i : i + 1, :] = to_row(column, eye)
        spread_block_row(blocks_ref, parts_ref, i, column)
    finish_spread(parts_ref, spread_ref, send_ref, z_ref[...], own_ref, packets)


def spread_kernel(
    turns,
    column_ref,
    row_ref,
    mine_ref,
    theirs_ref,
    solver_ref,
    null_ref,
    offset_ref,
    blocks_ref,
    spread_ref,
    send_ref,
    z_ref,
    own_ref,
    *refs,
):
    packets = refs[:turns]
    (parts_ref,) = refs[turns:]
    rows, width = z_ref.shape
    eye = eye_mask(width)
    coarse = coarse_field(mine_ref, theirs_ref, solver_ref, null_ref, offset_ref)
    z = row_ref[...] + coarse
    z_ref[...] = z
    for i in range(rows):
        column = column_ref[i][:, :width] + to_column(coarse[i : i + 1], eye)
        spread_block_row(blocks_ref, parts_ref, i, column)
    finish_spread(parts_ref, spread_ref, send_ref, z, own_ref, packets)


def apply_rows(arrived, z, own_ref, blocks_ref, pick_ref, back_ref, picked_ref):
    rows, width = z.shape
    slots = blocks_ref.shape[2]
    ghosts = arrived[0].shape[0] // 2
    eye = eye_mask(width)
    extended = jnp.concatenate([z] + [ref[0:ghosts, :] for ref in arrived], axis=0)
    picked_ref[...] = select_rows(pick_ref, extended)
    returned = jnp.concatenate([ref[ghosts:, :] for ref in arrived], axis=0)
    back = own_ref[...] + select_rows(back_ref, returned)
    image = []
    for i in range(rows):
        total = None
        for j in range(slots):
            at = i * slots + j
            term = blocks_ref[0, i, j] * picked_ref[at : at + 1, :]
            total = term if total is None else total + term
        column = jnp.sum(total, axis=1, keepdims=True)
        image.append(to_row(column, eye))
    return 0.5 * (jnp.concatenate(image, axis=0) + back)


def apply_kernel(turns, field_ref, z_ref, own_ref, *refs):
    arrived = refs[:turns]
    (
        blocks_ref,
        pick_ref,
        back_ref,
        null_ref,
        offset_ref,
        next_ref,
        coarse_ref,
        picked_ref,
    ) = refs[turns:]
    image = apply_rows(arrived, z_ref[...], own_ref, blocks_ref, pick_ref, back_ref, picked_ref)
    following = image - SHIFT * field_ref[...].reshape(image.shape)
    next_ref[...] = following
    coarse_ref[...] = restrict(null_ref, offset_ref, following)


def last_kernel(turns, fields, *refs):
    field_refs = refs[:fields]
    z_refs = refs[fields : 2 * fields]
    own_ref = refs[2 * fields]
    arrived = refs[2 * fields + 1 : 2 * fields + 1 + turns]
    blocks_ref, pick_ref, back_ref, next_ref, dots_ref, picked_ref = refs[2 * fields + 1 + turns :]
    image = apply_rows(
        arrived, z_refs[-1][...], own_ref, blocks_ref, pick_ref, back_ref, picked_ref
    )
    following = image - SHIFT * field_refs[-1][...]
    next_ref[...] = following
    lane = lax.broadcasted_iota(jnp.int32, (1, 128), 1)
    values = [ref[...].reshape(image.shape) for ref in field_refs] + [following]
    packed = jnp.zeros((1, 128), f32)
    for a, value in enumerate(values):
        for c, z_at in enumerate(z_refs):
            column = jnp.sum(value * z_at[...], axis=0, keepdims=True)
            dot = jnp.sum(column, axis=1, keepdims=True)
            packed = jnp.where(lane == a * fields + c, dot, packed)
    dots_ref[...] = jnp.broadcast_to(packed.reshape(1, 1, 128), dots_ref.shape)


def finish_kernel(fields, dots_ref, *refs):
    value_refs = refs[: fields + 1]
    z_refs = refs[fields + 1 : 2 * fields + 1]
    solution_ref, residual_ref = refs[2 * fields + 1 :]
    total = jnp.sum(dots_ref[...], axis=0)
    lane = lax.broadcasted_iota(jnp.int32, (1, 128), 1)
    shape = solution_ref.shape[1:]
    gram = [
        [
            jnp.sum(jnp.where(lane == a * fields + c, total, 0.0), axis=1, keepdims=True)
            for c in range(fields)
        ]
        for a in range(fields + 1)
    ]
    zero = jnp.zeros((1, 1), f32)
    one = jnp.ones((1, 1), f32)

    def form(left, right):
        value = zero
        for a, left_at in enumerate(left):
            if left_at is None:
                continue
            for c, right_at in enumerate(right):
                if right_at is not None:
                    value = value + left_at * right_at * gram[a][c]
        return value

    def plus(first, second):
        if first is None:
            return second
        return first if second is None else first + second

    def scaled(scale, value):
        return None if value is None else scale * value

    residual = [one] + [None] * fields
    direction = [one] + [None] * (fields - 1)
    iterate = [None] * fields
    product_now = form(residual, direction)
    for step in range(fields):
        image = [None] * (fields + 1)
        for c in range(fields):
            if direction[c] is not None:
                image[c] = plus(image[c], SHIFT * direction[c])
                image[c + 1] = plus(image[c + 1], direction[c])
        alpha = product_now / form(image, direction)
        iterate = [plus(iterate[c], scaled(alpha, direction[c])) for c in range(fields)]
        residual = [plus(residual[a], scaled(-alpha, image[a])) for a in range(fields + 1)]
        if step + 1 < fields:
            product_next = form(residual, residual[:fields])
            beta = product_next / product_now
            direction = [plus(residual[c], scaled(beta, direction[c])) for c in range(fields)]
            product_now = product_next
    answer = iterate[0] * z_refs[0][...]
    for c in range(1, fields):
        answer = answer + iterate[c] * z_refs[c][...]
    left_over = residual[0] * value_refs[0][...].reshape(shape)
    for a in range(1, fields + 1):
        left_over = left_over + residual[a] * value_refs[a][...]
    solution_ref[0] = answer
    residual_ref[0] = left_over


def on_device(
    right_side,
    blocks,
    pattern,
    send_rows,
    inverse_blocks,
    margin_blocks,
    near_null,
    aggregate,
    coarse_inverse,
):
    rows, width = right_side.shape[1:]
    slots = blocks.shape[2]
    turns, ghosts = send_rows.shape[1:]
    extent = rows + turns * ghosts
    modes = near_null.shape[2]
    levels = lax.axis_size("sub").bit_length() - 1
    bits = [turn * levels // turns for turn in range(turns)]
    devices = lax.axis_size("sub") * lax.axis_size("coarse")
    flip = [(0, 1), (1, 0)]
    row_shape = (rows, width)
    packet = (2 * ghosts, width)
    parts = rows * slots
    ghost_total = turns * ghosts
    parts_scratch = [pltpu.VMEM((parts, width), f32)]
    null_view = jnp.transpose(near_null, (0, 2, 1, 3))
    pattern_view = jnp.transpose(pattern, (2, 0, 1))

    def swap(array):
        return lax.ppermute(array, "coarse", flip)

    packs = call(
        pack_kernel,
        [(ghosts, width * width // 128, 128)] * turns,
        [VMEM] + [ANY] * REPEATS,
        [margin_blocks] * (1 + REPEATS),
        name="pack_margin",
    )
    gathered = [partner(packs[turn], "sub", bits[turn]) for turn in range(turns)]
    offset, mine = call(
        restrict_kernel,
        [((rows, 128), jnp.int32), (1, 128)],
        [VMEM, VMEM, SMEM],
        [right_side, null_view, aggregate],
        name="restrict",
    )
    theirs = swap(mine)
    pick, spread, send, back = call(
        table_kernel,
        [
            ((parts, 3 * extent), bf16),
            ((extent, 3 * parts), bf16),
            ((ghost_total, 3 * rows), bf16),
            ((rows, 3 * ghost_total), bf16),
        ],
        [SMEM, SMEM],
        [pattern_view, send_rows],
        scratch=[pltpu.VMEM((parts, 128), f32), pltpu.VMEM((ghost_total, 128), f32)],
        name="tables",
    )
    source, null_modes, held, solver = right_side, null_view, blocks, coarse_inverse
    combined, z, own, *packets = call(
        functools.partial(first_kernel, turns),
        [(rows, width, width), row_shape, row_shape] + [packet] * turns,
        [VMEM] * (turns + 10) + [SMEM],
        [source, inverse_blocks, *gathered[::-1], mine, theirs, solver, null_modes, offset, held, spread, send]
        + [send_rows],
        scratch=parts_scratch,
        name="first_spread",
    )
    values = [source]
    fields = [z]
    for step in range(ITERS):
        arrived = [partner(packets[turn], "sub", bits[turn]) for turn in range(turns)]
        if step + 1 == ITERS:
            break
        following, mine = call(
            functools.partial(apply_kernel, turns),
            [row_shape, (1, 128)],
            [VMEM] * (turns + 8),
            [values[-1], fields[-1], own, *arrived, held, pick, back, null_modes, offset],
            scratch=parts_scratch,
            name="apply",
        )
        values.append(following)
        theirs = swap(mine)
        column, row = call(
            local_kernel,
            [(rows, width, 128), row_shape],
            [VMEM, VMEM],
            [following, combined],
            name="local_inverse",
        )
        z, own, *packets = call(
            functools.partial(spread_kernel, turns),
            [row_shape, row_shape] + [packet] * turns,
            [VMEM] * 10,
            [column, row, mine, theirs, solver, null_modes, offset, held, spread, send],
            scratch=parts_scratch,
            name="spread",
        )
        fields.append(z)
    following, dots = call(
        functools.partial(last_kernel, turns, ITERS),
        [row_shape, (devices, 1, 128)],
        [VMEM] * (2 * ITERS + 1 + turns + 3),
        [*values, *fields, own, *arrived, held, pick, back],
        scratch=parts_scratch,
        name="last_apply",
    )
    values.append(following)
    exchanged = lax.all_to_all(dots, ("sub", "coarse"), 0, 0)
    answer, left_over = call(
        functools.partial(finish_kernel, ITERS),
        [right_side.shape] * 2,
        [VMEM] * (2 * ITERS + 2),
        [exchanged, *values, *fields],
        name="finish",
    )
    return answer, left_over


def solution(mesh):
    in_specs = (
        P("coarse", "sub", None),
        P("coarse", "sub", None, None, None),
        P("coarse", "sub", None),
        P("coarse", "sub", None),
        P("coarse", "sub", None, None),
        P("coarse", "sub", None, None),
        P("coarse", "sub", None, None),
        P("coarse", "sub"),
        P("sub", None, None),
    )
    out_specs = (P("coarse", "sub", None), P("coarse", "sub", None))
    return jax.shard_map(
        on_device, mesh=mesh, in_specs=in_specs, out_specs=out_specs, check_vma=False
    )
```

```python
import functools

import jax
import jax.numpy as jnp
from jax import lax
from jax.experimental import pallas as pl
from jax.experimental.pallas import tpu as pltpu
from jax.sharding import PartitionSpec as P

ITERS = 3
SHIFT = 2.0
REPEATS = 16

f32 = jnp.float32
bf16 = jnp.bfloat16
VMEM = pl.BlockSpec(memory_space=pltpu.VMEM)
ANY = pl.BlockSpec(memory_space=pl.ANY)
SMEM = pl.BlockSpec(memory_space=pltpu.SMEM)


def partner(array, axis, bit):
    return lax.ppermute(array, axis, [(i, i ^ 1 << bit) for i in range(lax.axis_size(axis))])


def call(kernel, outs, in_specs, args, scratch=(), name=None, cost=100000):
    return pl.pallas_call(
        kernel,
        out_shape=[
            jax.ShapeDtypeStruct(*(out if isinstance(out[0], tuple) else (out, f32))) for out in outs
        ],
        in_specs=in_specs,
        out_specs=[VMEM] * len(outs),
        scratch_shapes=list(scratch),
        compiler_params=pltpu.CompilerParams(vmem_limit_bytes=12 * 1024 * 1024),
        cost_estimate=pl.CostEstimate(flops=0, bytes_accessed=cost, transcendentals=0),
        name=name,
    )(*args)


def eye_mask(width):
    return lax.broadcasted_iota(jnp.int32, (width, width), 0) == lax.broadcasted_iota(
        jnp.int32, (width, width), 1
    )


def to_column(row, eye):
    return jnp.sum(jnp.where(eye, row, 0.0), axis=1, keepdims=True)


def to_row(column, eye):
    return jnp.sum(jnp.where(eye, column, 0.0), axis=0, keepdims=True)


def restrict(null_ref, offset_ref, field):
    offset = offset_ref[...]
    total = jnp.zeros(offset.shape, f32)
    for mode in range(null_ref.shape[1]):
        dots = jnp.sum(null_ref[0, mode] * field, axis=1, keepdims=True)
        total = total + jnp.where(offset == mode, dots, 0.0)
    return jnp.sum(total, axis=0, keepdims=True)


def coarse_field(mine_ref, theirs_ref, solver_ref, null_ref, offset_ref):
    size = solver_ref.shape[1]
    total = mine_ref[...] + theirs_ref[...]
    solved = jnp.sum(solver_ref[0] * total[:, :size], axis=1, keepdims=True)
    flat = to_row(solved, eye_mask(size))
    offset = offset_ref[:, :size]
    field = None
    for mode in range(null_ref.shape[1]):
        weight = jnp.sum(jnp.where(offset == mode, flat, 0.0), axis=1, keepdims=True)
        term = null_ref[0, mode] * weight
        field = term if field is None else field + term
    return field


def thirds(value):
    high = value.astype(bf16)
    rest = value - high.astype(f32)
    middle = rest.astype(bf16)
    low = (rest - middle.astype(f32)).astype(bf16)
    return jnp.concatenate([high, middle, low], axis=0)


def select_rows(table_ref, value):
    return jnp.dot(table_ref[...], thirds(value), preferred_element_type=f32)


def triple(table):
    return jnp.concatenate([table.astype(bf16)] * 3, axis=1)


def pack_kernel(margin_ref, *refs):
    outs = refs[REPEATS:]
    turns = len(outs)
    ghosts = margin_ref.shape[1] // turns
    width = margin_ref.shape[2]
    tall = width * width // 128
    side = 128 - width
    rest = width - tall
    for turn in range(turns):
        for g in range(ghosts):
            block = margin_ref[0, turn * ghosts + g]
            outs[turn][g, :, 0:width] = block[:tall]
            for piece in range(width // side):
                outs[turn][g, piece * rest : (piece + 1) * rest, width:128] = block[
                    tall:, piece * side : (piece + 1) * side
                ]


def restrict_kernel(field_ref, null_ref, aggregate_ref, offset_ref, mine_ref):
    modes = null_ref.shape[1]
    lane = lax.broadcasted_iota(jnp.int32, (1, 128), 1)
    for i in range(offset_ref.shape[0]):
        offset_ref[i : i + 1, :] = lane - aggregate_ref[0, i] * modes
    mine_ref[...] = restrict(null_ref, offset_ref, field_ref[0])


def table_kernel(
    pattern_ref, senders_ref, pick_ref, send_ref, back_ref, index_ref, table_ref, send_table_ref
):
    slots, _, rows = pattern_ref.shape
    turns, ghosts = senders_ref.shape[1:]
    extent = pick_ref.shape[1] // 3
    lane = lax.broadcasted_iota(jnp.int32, (1, 128), 1)
    columns = jnp.zeros((1, 128), jnp.int32)
    for i in range(rows):
        for j in range(slots):
            at = i * slots + j
            table_ref[at : at + 1, :] = jnp.where(lane == pattern_ref[j, 0, i], 1.0, 0.0)
            columns = jnp.where(lane == at, pattern_ref[j, 0, i], columns)
    index_ref[0:1, :] = columns
    sent = jnp.zeros((1, 128), jnp.int32)
    for turn in range(turns):
        for g in range(ghosts):
            at = turn * ghosts + g
            send_table_ref[at : at + 1, :] = jnp.where(lane == senders_ref[0, turn, g], 1.0, 0.0)
            sent = jnp.where(lane == at, senders_ref[0, turn, g], sent)
    index_ref[1:2, :] = sent
    table = table_ref[...]
    pick_ref[...] = triple(table[:, :extent])
    send_table = send_table_ref[...]
    send_ref[...] = triple(send_table[:, :rows])
    back_ref[...] = triple(send_table.T[:rows])


def local_kernel(field_ref, inverse_ref, column_ref, row_ref):
    rows, width = row_ref.shape
    field_ref = field_ref.reshape(rows, width)
    inverse_ref = inverse_ref.reshape(rows, width, width)
    eye = eye_mask(width)
    for i in range(rows):
        column = jnp.sum(inverse_ref[i] * field_ref[i : i + 1, :], axis=1, keepdims=True)
        column_ref[i] = jnp.broadcast_to(column, (width, 128))
        row_ref[i : i + 1, :] = to_row(column, eye)


def spread_block_row(blocks_ref, parts_ref, i, column):
    slots, width = blocks_ref.shape[2:4]
    for j in range(slots):
        part = blocks_ref[0, i, j, 0:8, :] * column[0:8]
        for start in range(8, width, 8):
            part = part + blocks_ref[0, i, j, start : start + 8, :] * column[start : start + 8]
        at = i * slots + j
        parts_ref[at : at + 1, :] = jnp.sum(part, axis=0, keepdims=True)


def finish_spread(parts_ref, slots_ref, indices_ref, z_ref, own_ref, packets):
    turns = len(packets)
    rows = z_ref.shape[0]
    ghosts = packets[0].shape[0] // 2
    slots = slots_ref.shape[0]
    for i in range(rows):
        slots_ref[0, i : i + 1, :] = parts_ref[i * slots : i * slots + 1, :]
        for j in range(1, slots):
            at = i * slots + j
            slots_ref[j, pl.ds(indices_ref[0, at], 1), :] = parts_ref[at : at + 1, :]
    for turn in range(turns):
        for g in range(ghosts):
            at = indices_ref[1, turn * ghosts + g]
            packets[turn][g : g + 1, :] = z_ref[pl.ds(at, 1), :]
    spread = slots_ref[0]
    for j in range(1, slots):
        spread = spread + slots_ref[j]
    own_ref[...] = spread[:rows]
    for turn in range(turns):
        start = rows + turn * ghosts
        packets[turn][ghosts:, :] = spread[start : start + ghosts]


def margin_row(packed_ref, g, row, eye):
    tall = packed_ref.shape[1]
    width = row.shape[1]
    side = 128 - width
    rest = width - tall
    column = jnp.sum(packed_ref[g, :, 0:width] * row, axis=1, keepdims=True)
    beside = jnp.zeros((rest, side), f32)
    for piece in range(width // side):
        beside = (
            beside
            + packed_ref[g, piece * rest : (piece + 1) * rest, width:128]
            * row[:, piece * side : (piece + 1) * side]
        )
    beside = jnp.sum(beside, axis=1, keepdims=True)
    return to_row(column, eye[:tall]) + to_row(beside, eye[tall:])


def margin_kernel(turns, field_ref, send_ref, *refs):
    early = refs[:turns][::-1]
    out_ref, picked_ref = refs[turns:]
    ghosts = early[0].shape[0]
    eye = eye_mask(out_ref.shape[1])
    picked_ref[...] = select_rows(send_ref, field_ref[0])
    first = out_ref.shape[0] // ghosts - turns
    out_ref[...] = picked_ref[...]
    for turn in range(turns):
        for g in range(ghosts):
            at = (first + turn) * ghosts + g
            out_ref[at : at + 1, :] = margin_row(early[turn], g, picked_ref[at : at + 1, :], eye)


def combine_kernel(turns, inverse_ref, senders_ref, *refs):
    gathered = refs[:turns]
    (combined_ref,) = refs[turns:]
    ghosts, tall = gathered[0].shape[:2]
    width = inverse_ref.shape[2]
    side = 128 - width
    rest = width - tall
    combined_ref[...] = inverse_ref[0]
    for turn in range(turns):
        for g in range(ghosts):
            at = senders_ref[0, turn, g]
            combined_ref[at, 0:tall, :] += gathered[turn][g, :, 0:width]
            for piece in range(width // side):
                combined_ref[at, tall:, piece * side : (piece + 1) * side] += gathered[turn][
                    g, piece * rest : (piece + 1) * rest, width:128
                ]


def first_kernel(turns, column_ref, row_ref, margin_ref, late_ref, *refs):
    (
        mine_ref,
        theirs_ref,
        solver_ref,
        null_ref,
        offset_ref,
        back_ref,
        blocks_ref,
        index_ref,
        z_ref,
        own_ref,
    ) = refs[:10]
    packets = refs[10 : turns + 10]
    parts_ref, slots_ref, indices_ref, sem = refs[turns + 10 :]
    fetch = pltpu.make_async_copy(index_ref, indices_ref, sem)
    fetch.start()
    slots_ref[...] = jnp.zeros(slots_ref.shape, f32)
    rows, width = z_ref.shape
    ghosts = late_ref.shape[0]
    eye = eye_mask(width)
    late = [margin_row(late_ref, g, margin_ref[g : g + 1, :], eye) for g in range(ghosts)]
    margin = jnp.concatenate(late + [margin_ref[ghosts:, :]], axis=0)
    coarse = coarse_field(mine_ref, theirs_ref, solver_ref, null_ref, offset_ref)
    added = coarse + select_rows(back_ref, margin)
    z = row_ref[...] + added
    z_ref[...] = z
    for i in range(rows):
        column = column_ref[i][:, :width] + to_column(added[i : i + 1], eye)
        spread_block_row(blocks_ref, parts_ref, i, column)
    fetch.wait()
    finish_spread(parts_ref, slots_ref, indices_ref, z_ref, own_ref, packets)


def spread_kernel(
    turns,
    column_ref,
    row_ref,
    mine_ref,
    theirs_ref,
    solver_ref,
    null_ref,
    offset_ref,
    blocks_ref,
    index_ref,
    z_ref,
    own_ref,
    *refs,
):
    packets = refs[:turns]
    parts_ref, slots_ref, indices_ref, sem = refs[turns:]
    fetch = pltpu.make_async_copy(index_ref, indices_ref, sem)
    fetch.start()
    slots_ref[...] = jnp.zeros(slots_ref.shape, f32)
    rows, width = z_ref.shape
    eye = eye_mask(width)
    coarse = coarse_field(mine_ref, theirs_ref, solver_ref, null_ref, offset_ref)
    z = row_ref[...] + coarse
    z_ref[...] = z
    for i in range(rows):
        column = column_ref[i][:, :width] + to_column(coarse[i : i + 1], eye)
        spread_block_row(blocks_ref, parts_ref, i, column)
    fetch.wait()
    finish_spread(parts_ref, slots_ref, indices_ref, z_ref, own_ref, packets)


def apply_rows(arrived, z, own_ref, blocks_ref, pick_ref, back_ref, picked_ref):
    rows, width = z.shape
    slots = blocks_ref.shape[2]
    ghosts = arrived[0].shape[0] // 2
    eye = eye_mask(width)
    extended = jnp.concatenate([z] + [ref[0:ghosts, :] for ref in arrived], axis=0)
    picked_ref[...] = select_rows(pick_ref, extended)
    returned = jnp.concatenate([ref[ghosts:, :] for ref in arrived], axis=0)
    back = own_ref[...] + select_rows(back_ref, returned)
    image = []
    for i in range(rows):
        total = None
        for j in range(slots):
            at = i * slots + j
            term = blocks_ref[0, i, j] * picked_ref[at : at + 1, :]
            total = term if total is None else total + term
        column = jnp.sum(total, axis=1, keepdims=True)
        image.append(to_row(column, eye))
    return 0.5 * (jnp.concatenate(image, axis=0) + back)


def apply_kernel(turns, field_ref, z_ref, own_ref, *refs):
    arrived = refs[:turns][::-1]
    (
        blocks_ref,
        pick_ref,
        back_ref,
        null_ref,
        offset_ref,
        next_ref,
        coarse_ref,
        picked_ref,
    ) = refs[turns:]
    image = apply_rows(arrived, z_ref[...], own_ref, blocks_ref, pick_ref, back_ref, picked_ref)
    following = image - SHIFT * field_ref[...].reshape(image.shape)
    next_ref[...] = following
    coarse_ref[...] = restrict(null_ref, offset_ref, following)


def last_kernel(turns, fields, *refs):
    field_refs = refs[:fields]
    z_refs = refs[fields : 2 * fields]
    own_ref = refs[2 * fields]
    arrived = refs[2 * fields + 1 : 2 * fields + 1 + turns][::-1]
    blocks_ref, pick_ref, back_ref, next_ref, dots_ref, picked_ref = refs[2 * fields + 1 + turns :]
    image = apply_rows(
        arrived, z_refs[-1][...], own_ref, blocks_ref, pick_ref, back_ref, picked_ref
    )
    following = image - SHIFT * field_refs[-1][...]
    next_ref[...] = following
    lane = lax.broadcasted_iota(jnp.int32, (1, 128), 1)
    values = [ref[...].reshape(image.shape) for ref in field_refs] + [following]
    packed = jnp.zeros((1, 128), f32)
    for a, value in enumerate(values):
        for c, z_at in enumerate(z_refs):
            column = jnp.sum(value * z_at[...], axis=0, keepdims=True)
            dot = jnp.sum(column, axis=1, keepdims=True)
            packed = jnp.where(lane == a * fields + c, dot, packed)
    dots_ref[...] = jnp.broadcast_to(packed.reshape(1, 1, 128), dots_ref.shape)


def finish_kernel(fields, dots_ref, *refs):
    value_refs = refs[: fields + 1]
    z_refs = refs[fields + 1 : 2 * fields + 1]
    solution_ref, residual_ref = refs[2 * fields + 1 :]
    total = jnp.sum(dots_ref[...], axis=0)
    lane = lax.broadcasted_iota(jnp.int32, (1, 128), 1)
    shape = solution_ref.shape[1:]
    gram = [
        [
            jnp.sum(jnp.where(lane == a * fields + c, total, 0.0), axis=1, keepdims=True)
            for c in range(fields)
        ]
        for a in range(fields + 1)
    ]
    zero = jnp.zeros((1, 1), f32)
    one = jnp.ones((1, 1), f32)

    def form(left, right):
        value = zero
        for a, left_at in enumerate(left):
            if left_at is None:
                continue
            for c, right_at in enumerate(right):
                if right_at is not None:
                    value = value + left_at * right_at * gram[a][c]
        return value

    def plus(first, second):
        if first is None:
            return second
        return first if second is None else first + second

    def scaled(scale, value):
        return None if value is None else scale * value

    residual = [one] + [None] * fields
    direction = [one] + [None] * (fields - 1)
    iterate = [None] * fields
    product_now = form(residual, direction)
    for step in range(fields):
        image = [None] * (fields + 1)
        for c in range(fields):
            if direction[c] is not None:
                image[c] = plus(image[c], SHIFT * direction[c])
                image[c + 1] = plus(image[c + 1], direction[c])
        alpha = product_now / form(image, direction)
        iterate = [plus(iterate[c], scaled(alpha, direction[c])) for c in range(fields)]
        residual = [plus(residual[a], scaled(-alpha, image[a])) for a in range(fields + 1)]
        if step + 1 < fields:
            product_next = form(residual, residual[:fields])
            beta = product_next / product_now
            direction = [plus(residual[c], scaled(beta, direction[c])) for c in range(fields)]
            product_now = product_next
    answer = iterate[0] * z_refs[0][...]
    for c in range(1, fields):
        answer = answer + iterate[c] * z_refs[c][...]
    left_over = residual[0] * value_refs[0][...].reshape(shape)
    for a in range(1, fields + 1):
        left_over = left_over + residual[a] * value_refs[a][...]
    solution_ref[0] = answer
    residual_ref[0] = left_over


def on_device(
    right_side,
    blocks,
    pattern,
    send_rows,
    inverse_blocks,
    margin_blocks,
    near_null,
    aggregate,
    coarse_inverse,
):
    rows, width = right_side.shape[1:]
    slots = blocks.shape[2]
    turns, ghosts = send_rows.shape[1:]
    extent = rows + turns * ghosts
    modes = near_null.shape[2]
    levels = lax.axis_size("sub").bit_length() - 1
    bits = [turn * levels // turns for turn in range(turns)]
    devices = lax.axis_size("sub") * lax.axis_size("coarse")
    flip = [(0, 1), (1, 0)]
    row_shape = (rows, width)
    packet = (2 * ghosts, width)
    parts = rows * slots
    ghost_total = turns * ghosts
    parts_scratch = [pltpu.VMEM((parts, width), f32)]
    spread_scratch = parts_scratch + [
        pltpu.VMEM((slots, extent, width), f32),
        pltpu.SMEM((2, 128), jnp.int32),
        pltpu.SemaphoreType.DMA,
    ]
    null_view = jnp.transpose(near_null, (0, 2, 1, 3))
    pattern_view = jnp.transpose(pattern, (2, 0, 1))

    def swap(array):
        return lax.ppermute(array, "coarse", flip)

    packs = call(
        pack_kernel,
        [(ghosts, width * width // 128, 128)] * turns,
        [VMEM] + [ANY] * REPEATS,
        [margin_blocks] * (1 + REPEATS),
        name="pack_margin",
    )
    gathered = [partner(packs[turn], "sub", bits[turn]) for turn in range(turns)]
    offset, mine = call(
        restrict_kernel,
        [((rows, 128), jnp.int32), (1, 128)],
        [VMEM, VMEM, SMEM],
        [right_side, null_view, aggregate],
        name="restrict",
    )
    theirs = swap(mine)
    pick, send, back, index = call(
        table_kernel,
        [
            ((parts, 3 * extent), bf16),
            ((ghost_total, 3 * rows), bf16),
            ((rows, 3 * ghost_total), bf16),
            ((2, 128), jnp.int32),
        ],
        [SMEM, SMEM],
        [pattern_view, send_rows],
        scratch=[pltpu.VMEM((parts, 128), f32), pltpu.VMEM((ghost_total, 128), f32)],
        name="tables",
    )
    source, null_modes, held, solver = right_side, null_view, blocks, coarse_inverse
    column, row = call(
        local_kernel,
        [(rows, width, 128), row_shape],
        [VMEM, VMEM],
        [right_side, inverse_blocks],
        name="local_inverse",
    )
    (margin,) = call(
        functools.partial(margin_kernel, turns - 1),
        [(ghost_total, width)],
        [VMEM] * (turns + 1),
        [source, send, *gathered[:0:-1]],
        scratch=[pltpu.VMEM((ghost_total, width), f32)],
        name="margin_rows",
    )
    z, own, *packets = call(
        functools.partial(first_kernel, turns),
        [row_shape, row_shape] + [packet] * turns,
        [VMEM] * 12,
        [column, row, margin, gathered[0], mine, theirs, solver, null_modes, offset, back]
        + [held, index],
        scratch=spread_scratch,
        name="first_spread",
    )
    (combined,) = call(
        functools.partial(combine_kernel, turns),
        [(rows, width, width)],
        [VMEM, SMEM] + [VMEM] * turns,
        [inverse_blocks, send_rows, *gathered],
        name="combine",
    )
    values = [source]
    fields = [z]
    for step in range(ITERS):
        arrived = [partner(packets[turn], "sub", bits[turn]) for turn in range(turns)]
        if step == 0:
            combined, *arrived = lax.optimization_barrier([combined, *arrived[::-1]])
            arrived = arrived[::-1]
        if step + 1 == ITERS:
            break
        following, mine = call(
            functools.partial(apply_kernel, turns),
            [row_shape, (1, 128)],
            [VMEM] * (turns + 8),
            [values[-1], fields[-1], own, *arrived[::-1], held, pick, back, null_modes, offset],
            scratch=parts_scratch,
            name="apply",
        )
        values.append(following)
        theirs = swap(mine)
        column, row = call(
            local_kernel,
            [(rows, width, 128), row_shape],
            [VMEM, VMEM],
            [following, combined],
            name="local_inverse",
        )
        z, own, *packets = call(
            functools.partial(spread_kernel, turns),
            [row_shape, row_shape] + [packet] * turns,
            [VMEM] * 9,
            [column, row, mine, theirs, solver, null_modes, offset, held, index],
            scratch=spread_scratch,
            name="spread",
        )
        fields.append(z)
    following, dots = call(
        functools.partial(last_kernel, turns, ITERS),
        [row_shape, (devices, 1, 128)],
        [VMEM] * (2 * ITERS + 1 + turns + 3),
        [*values, *fields, own, *arrived[::-1], held, pick, back],
        scratch=parts_scratch,
        name="last_apply",
    )
    values.append(following)
    exchanged = lax.all_to_all(dots, ("sub", "coarse"), 0, 0)
    answer, left_over = call(
        functools.partial(finish_kernel, ITERS),
        [right_side.shape] * 2,
        [VMEM] * (2 * ITERS + 2),
        [exchanged, *values, *fields],
        name="finish",
    )
    return answer, left_over


def solution(mesh):
    in_specs = (
        P("coarse", "sub", None),
        P("coarse", "sub", None, None, None),
        P("coarse", "sub", None),
        P("coarse", "sub", None),
        P("coarse", "sub", None, None),
        P("coarse", "sub", None, None),
        P("coarse", "sub", None, None),
        P("coarse", "sub"),
        P("sub", None, None),
    )
    out_specs = (P("coarse", "sub", None), P("coarse", "sub", None))
    return jax.shard_map(
        on_device, mesh=mesh, in_specs=in_specs, out_specs=out_specs, check_vma=False
    )
```

```python
import functools

import jax
import jax.numpy as jnp
from jax import lax
from jax.experimental import pallas as pl
from jax.experimental.pallas import tpu as pltpu
from jax.sharding import PartitionSpec as P

ITERS = 3
SHIFT = 2.0
REPEATS = 16

f32 = jnp.float32
bf16 = jnp.bfloat16
VMEM = pl.BlockSpec(memory_space=pltpu.VMEM)
ANY = pl.BlockSpec(memory_space=pl.ANY)
SMEM = pl.BlockSpec(memory_space=pltpu.SMEM)


def partner(array, axis, bit):
    return lax.ppermute(array, axis, [(i, i ^ 1 << bit) for i in range(lax.axis_size(axis))])


def call(kernel, outs, in_specs, args, scratch=(), name=None, cost=100000):
    return pl.pallas_call(
        kernel,
        out_shape=[
            jax.ShapeDtypeStruct(*(out if isinstance(out[0], tuple) else (out, f32))) for out in outs
        ],
        in_specs=in_specs,
        out_specs=[VMEM] * len(outs),
        scratch_shapes=list(scratch),
        compiler_params=pltpu.CompilerParams(vmem_limit_bytes=12 * 1024 * 1024),
        cost_estimate=pl.CostEstimate(flops=0, bytes_accessed=cost, transcendentals=0),
        name=name,
    )(*args)


def eye_mask(width):
    return lax.broadcasted_iota(jnp.int32, (width, width), 0) == lax.broadcasted_iota(
        jnp.int32, (width, width), 1
    )


def to_column(row, eye):
    return jnp.sum(jnp.where(eye, row, 0.0), axis=1, keepdims=True)


def to_row(column, eye):
    return jnp.sum(jnp.where(eye, column, 0.0), axis=0, keepdims=True)


def restrict(null_ref, offset_ref, field):
    offset = offset_ref[...]
    total = jnp.zeros(offset.shape, f32)
    for mode in range(null_ref.shape[1]):
        dots = jnp.sum(null_ref[0, mode] * field, axis=1, keepdims=True)
        total = total + jnp.where(offset == mode, dots, 0.0)
    return jnp.sum(total, axis=0, keepdims=True)


def coarse_field(mine_ref, theirs_ref, solver_ref, null_ref, offset_ref):
    size = solver_ref.shape[1]
    total = mine_ref[...] + theirs_ref[...]
    solved = jnp.sum(solver_ref[0] * total[:, :size], axis=1, keepdims=True)
    flat = to_row(solved, eye_mask(size))
    offset = offset_ref[:, :size]
    field = None
    for mode in range(null_ref.shape[1]):
        weight = jnp.sum(jnp.where(offset == mode, flat, 0.0), axis=1, keepdims=True)
        term = null_ref[0, mode] * weight
        field = term if field is None else field + term
    return field


def thirds(value):
    high = value.astype(bf16)
    rest = value - high.astype(f32)
    middle = rest.astype(bf16)
    low = (rest - middle.astype(f32)).astype(bf16)
    return jnp.concatenate([high, middle, low], axis=0)


def select_rows(table_ref, value):
    return jnp.dot(table_ref[...], thirds(value), preferred_element_type=f32)


def triple(table):
    return jnp.concatenate([table.astype(bf16)] * 3, axis=1)


def pack_kernel(margin_ref, *refs):
    outs = refs[REPEATS:]
    turns = len(outs)
    ghosts, _, _ = outs[0].shape
    width = margin_ref.shape[2]
    tall = width * width // 128
    side = 128 - width
    rest = width - tall
    for turn in range(turns):
        for g in range(ghosts):
            block = margin_ref[0, turn * ghosts + g]
            outs[turn][g, :, 0:width] = block[:tall]
            for piece in range(width // side):
                outs[turn][g, piece * rest : (piece + 1) * rest, width:128] = block[
                    tall:, piece * side : (piece + 1) * side
                ]


def restrict_kernel(field_ref, null_ref, aggregate_ref, offset_ref, mine_ref):
    modes = null_ref.shape[1]
    lane = lax.broadcasted_iota(jnp.int32, (1, 128), 1)
    for i in range(offset_ref.shape[0]):
        offset_ref[i : i + 1, :] = lane - aggregate_ref[0, i] * modes
    mine_ref[...] = restrict(null_ref, offset_ref, field_ref[0])


def table_kernel(
    pattern_ref, senders_ref, pick_ref, send_ref, back_ref, index_ref, table_ref, send_table_ref
):
    slots, _, rows = pattern_ref.shape
    turns, ghosts = senders_ref.shape[1:]
    extent = pick_ref.shape[1] // 3
    lane = lax.broadcasted_iota(jnp.int32, (1, 128), 1)
    columns = jnp.zeros((1, 128), jnp.int32)
    for i in range(rows):
        for j in range(slots):
            at = i * slots + j
            table_ref[at : at + 1, :] = jnp.where(lane == pattern_ref[j, 0, i], 1.0, 0.0)
            columns = jnp.where(lane == at, pattern_ref[j, 0, i], columns)
    index_ref[0:1, :] = columns
    sent = jnp.zeros((1, 128), jnp.int32)
    for turn in range(turns):
        for g in range(ghosts):
            at = turn * ghosts + g
            send_table_ref[at : at + 1, :] = jnp.where(lane == senders_ref[0, turn, g], 1.0, 0.0)
            sent = jnp.where(lane == at, senders_ref[0, turn, g], sent)
    index_ref[1:2, :] = sent
    table = table_ref[...]
    pick_ref[...] = triple(table[:, :extent])
    send_table = send_table_ref[...]
    send_ref[...] = triple(send_table[:, :rows])
    back_ref[...] = triple(send_table.T[:rows])


def local_kernel(field_ref, inverse_ref, column_ref, row_ref):
    rows, width = row_ref.shape
    field_ref = field_ref.reshape(rows, width)
    inverse_ref = inverse_ref.reshape(rows, width, width)
    eye = eye_mask(width)
    for i in range(rows):
        column = jnp.sum(inverse_ref[i] * field_ref[i : i + 1, :], axis=1, keepdims=True)
        column_ref[i] = jnp.broadcast_to(column, (width, 128))
        row_ref[i : i + 1, :] = to_row(column, eye)


def spread_block_row(blocks_ref, parts_ref, i, column):
    slots, width = blocks_ref.shape[2:4]
    for j in range(slots):
        part = blocks_ref[0, i, j, 0:8, :] * column[0:8]
        for start in range(8, width, 8):
            part = part + blocks_ref[0, i, j, start : start + 8, :] * column[start : start + 8]
        at = i * slots + j
        parts_ref[at : at + 1, :] = jnp.sum(part, axis=0, keepdims=True)


def scatter_rows(parts_ref, slots_ref, indices_ref, rows):
    slots = slots_ref.shape[0]
    for i in range(rows):
        slots_ref[0, i : i + 1, :] = parts_ref[i * slots : i * slots + 1, :]
        for j in range(1, slots):
            at = i * slots + j
            slots_ref[j, pl.ds(indices_ref[0, at], 1), :] = parts_ref[at : at + 1, :]
    spread = slots_ref[0]
    for j in range(1, slots):
        spread = spread + slots_ref[j]
    return spread


def finish_spread(parts_ref, slots_ref, indices_ref, z_ref, own_ref, packets):
    turns = len(packets)
    rows = z_ref.shape[0]
    ghosts = packets[0].shape[0] // 2
    spread = scatter_rows(parts_ref, slots_ref, indices_ref, rows)
    own_ref[...] = spread[:rows]
    for turn in range(turns):
        for g in range(ghosts):
            at = indices_ref[1, turn * ghosts + g]
            packets[turn][g : g + 1, :] = z_ref[pl.ds(at, 1), :]
        start = rows + turn * ghosts
        packets[turn][ghosts:, :] = spread[start : start + ghosts]


def margin_row(packed_ref, g, wide_ref, at, eye, inside):
    pieces = wide_ref.shape[0]
    tall = packed_ref.shape[1]
    rest = tall // pieces
    products = [
        packed_ref[g, piece * rest : (piece + 1) * rest, :] * wide_ref[piece, at : at + 1, :]
        for piece in range(pieces)
    ]
    beside = products[0]
    for product in products[1:]:
        beside = beside + product
    main = [jnp.where(inside, product, 0.0) for product in products]
    columns = [jnp.sum(part, axis=1, keepdims=True) for part in main]
    columns.append(jnp.sum(jnp.where(inside, 0.0, beside), axis=1, keepdims=True))
    row = None
    for piece, column in enumerate(columns):
        part = jnp.where(eye[piece * rest : (piece + 1) * rest], column, 0.0)
        row = part if row is None else row + part
    return jnp.sum(row, axis=0, keepdims=True)


def margin_rows(packed, wide_ref, eye):
    ghosts = packed[0].shape[0]
    width = eye.shape[0]
    inside = lax.broadcasted_iota(jnp.int32, (1, 128), 1) < width
    out = []
    for turn, ref in enumerate(packed):
        for g in range(ghosts):
            out.append(margin_row(ref, g, wide_ref, turn * ghosts + g, eye, inside))
    return jnp.concatenate(out, axis=0)


def base_kernel(
    field_ref,
    send_ref,
    row_ref,
    mine_ref,
    theirs_ref,
    solver_ref,
    null_ref,
    offset_ref,
    base_ref,
    wide_ref,
):
    picked = select_rows(send_ref, field_ref[0])
    width = picked.shape[1]
    side = 128 - width
    for piece in range(wide_ref.shape[0]):
        wide_ref[piece, :, :width] = picked
        wide_ref[piece, :, width:] = picked[:, piece * side : (piece + 1) * side]
    coarse = coarse_field(mine_ref, theirs_ref, solver_ref, null_ref, offset_ref)
    base_ref[...] = row_ref[...] + coarse


def combine_kernel(turns, inverse_ref, senders_ref, *refs):
    gathered = refs[:turns]
    (combined_ref,) = refs[turns:]
    ghosts, tall = gathered[0].shape[:2]
    width = inverse_ref.shape[2]
    side = 128 - width
    rest = width - tall
    combined_ref[...] = inverse_ref[0]
    for turn in range(turns):
        for g in range(ghosts):
            at = senders_ref[0, turn, g]
            combined_ref[at, 0:tall, :] += gathered[turn][g, :, 0:width]
            for piece in range(width // side):
                combined_ref[at, tall:, piece * side : (piece + 1) * side] += gathered[turn][
                    g, piece * rest : (piece + 1) * rest, width:128
                ]


def first_kernel(turns, *refs):
    packed = refs[:turns][::-1]
    base_ref, wide_ref, back_ref, blocks_ref, index_ref, z_ref, own_ref = refs[turns : turns + 7]
    packets = refs[turns + 7 : 2 * turns + 7]
    parts_ref, slots_ref, indices_ref, sem = refs[2 * turns + 7 :]
    fetch = pltpu.make_async_copy(index_ref, indices_ref, sem)
    fetch.start()
    slots_ref[...] = jnp.zeros(slots_ref.shape, f32)
    rows, width = z_ref.shape
    eye = eye_mask(width)
    margin = margin_rows(packed, wide_ref, eye)
    z = base_ref[...] + select_rows(back_ref, margin)
    z_ref[...] = z
    for i in range(rows):
        spread_block_row(blocks_ref, parts_ref, i, to_column(z[i : i + 1], eye))
    fetch.wait()
    finish_spread(parts_ref, slots_ref, indices_ref, z_ref, own_ref, packets)


def spread_rows(
    column_ref,
    row_ref,
    mine_ref,
    theirs_ref,
    solver_ref,
    null_ref,
    offset_ref,
    blocks_ref,
    z_ref,
    parts_ref,
):
    rows, width = z_ref.shape
    eye = eye_mask(width)
    coarse = coarse_field(mine_ref, theirs_ref, solver_ref, null_ref, offset_ref)
    z_ref[...] = row_ref[...] + coarse
    for i in range(rows):
        column = column_ref[i][:, :width] + to_column(coarse[i : i + 1], eye)
        spread_block_row(blocks_ref, parts_ref, i, column)


def spread_kernel(turns, *refs):
    index_ref, z_ref, own_ref = refs[8:11]
    packets = refs[11 : 11 + turns]
    parts_ref, slots_ref, indices_ref, sem = refs[11 + turns :]
    fetch = pltpu.make_async_copy(index_ref, indices_ref, sem)
    fetch.start()
    slots_ref[...] = jnp.zeros(slots_ref.shape, f32)
    spread_rows(*refs[:8], z_ref, parts_ref)
    fetch.wait()
    finish_spread(parts_ref, slots_ref, indices_ref, z_ref, own_ref, packets)


def dot_at(lane, at, first, second, packed):
    dot = jnp.sum(jnp.sum(first * second, axis=0, keepdims=True), axis=1, keepdims=True)
    return jnp.where(lane == at, dot, packed)


def early_dots_kernel(fields, *refs):
    value_refs = refs[:fields]
    z_refs = refs[fields:-1]
    rows, width = z_refs[0].shape
    lane = lax.broadcasted_iota(jnp.int32, (1, 128), 1)
    packed = jnp.zeros((1, 128), f32)
    for a in range(fields):
        value = value_refs[a][...].reshape(rows, width)
        for c, z_at in enumerate(z_refs):
            packed = dot_at(lane, width + a * fields + c, value, z_at[...], packed)
    refs[-1][...] = packed


def last_spread_kernel(fields, *refs):
    index_ref, early_ref = refs[8:10]
    value_refs = refs[10 : 10 + fields]
    z_ref, own_ref, payload_ref, parts_ref, slots_ref, line_ref, indices_ref, sem = refs[10 + fields :]
    fetch = pltpu.make_async_copy(index_ref, indices_ref, sem)
    fetch.start()
    slots_ref[...] = jnp.zeros(slots_ref.shape, f32)
    line_ref[...] = jnp.zeros(line_ref.shape, f32)
    spread_rows(*refs[:8], z_ref, parts_ref)
    rows, width = z_ref.shape
    ghosts = line_ref.shape[0] // 2
    z = z_ref[...]
    lane = lax.broadcasted_iota(jnp.int32, (1, 128), 1)
    packed = early_ref[...]
    for a in range(fields):
        value = value_refs[a][...].reshape(rows, width)
        packed = dot_at(lane, width + a * fields + fields - 1, value, z, packed)
    fetch.wait()
    spread = scatter_rows(parts_ref, slots_ref, indices_ref, rows)
    own = spread[:rows]
    own_ref[...] = own
    packed = dot_at(lane, width + fields * fields, z, own, packed)
    line_ref[0:1, :] = packed
    line_ref[0:ghosts, :width] = spread[rows:]
    for at in range(ghosts):
        line_ref[ghosts + at : ghosts + at + 1, :width] = z_ref[pl.ds(indices_ref[1, at], 1), :]
    line = line_ref[...]
    for device in range(payload_ref.shape[0]):
        payload_ref[device] = line


def total_kernel(bits, fields, width, lines_ref, out_ref):
    devices, height = lines_ref.shape[:2]
    ghosts = height // 2
    each = ghosts // len(bits)
    lane = lax.broadcasted_iota(jnp.int32, (1, 128), 1)
    packed = lines_ref[0, 0:1, :]
    for device in range(1, devices):
        packed = packed + lines_ref[device, 0:1, :]
    crossed = jnp.zeros((each, 128), f32)
    for device in range(devices):
        for turn, bit in enumerate(bits):
            start = turn * each
            crossed = crossed + (
                lines_ref[device, start : start + each, :]
                * lines_ref[device ^ (1 << bit), ghosts + start : ghosts + start + each, :]
            )
    crossed = jnp.where(lane < width, jnp.sum(crossed, axis=0, keepdims=True), 0.0)
    crossed = jnp.sum(crossed, axis=1, keepdims=True)
    at = lane == width + fields * fields
    out_ref[...] = packed + jnp.where(at, crossed, 0.0)


def apply_rows(rims, returned, z, own_ref, blocks_ref, pick_ref, back_ref, picked_ref):
    rows, width = z.shape
    slots = blocks_ref.shape[2]
    eye = eye_mask(width)
    extended = jnp.concatenate([z] + rims, axis=0)
    picked_ref[...] = select_rows(pick_ref, extended)
    returned = jnp.concatenate(returned, axis=0)
    back = own_ref[...] + select_rows(back_ref, returned)
    image = []
    for i in range(rows):
        total = None
        for j in range(slots):
            at = i * slots + j
            term = blocks_ref[0, i, j] * picked_ref[at : at + 1, :]
            total = term if total is None else total + term
        column = jnp.sum(total, axis=1, keepdims=True)
        image.append(to_row(column, eye))
    return 0.5 * (jnp.concatenate(image, axis=0) + back)


def apply_kernel(turns, field_ref, z_ref, own_ref, *refs):
    arrived = refs[:turns][::-1]
    (
        blocks_ref,
        pick_ref,
        back_ref,
        null_ref,
        offset_ref,
        next_ref,
        coarse_ref,
        picked_ref,
    ) = refs[turns:]
    ghosts = arrived[0].shape[0] // 2
    rims = [ref[0:ghosts, :] for ref in arrived]
    returned = [ref[ghosts:, :] for ref in arrived]
    image = apply_rows(
        rims, returned, z_ref[...], own_ref, blocks_ref, pick_ref, back_ref, picked_ref
    )
    following = image - SHIFT * field_ref[...].reshape(image.shape)
    next_ref[...] = following
    coarse_ref[...] = restrict(null_ref, offset_ref, following)


def last_kernel(
    bits,
    field_ref,
    z_ref,
    own_ref,
    lines_ref,
    blocks_ref,
    pick_ref,
    back_ref,
    next_ref,
    picked_ref,
):
    width = z_ref.shape[1]
    ghosts = lines_ref.shape[1] // 2
    each = ghosts // len(bits)
    here = lax.axis_index("sub")
    rims = []
    returned = []
    for turn, bit in enumerate(bits):
        start = turn * each
        there = jnp.bitwise_xor(here, 1 << bit)
        returned.append(lines_ref[there, start : start + each, :width])
        rims.append(lines_ref[there, ghosts + start : ghosts + start + each, :width])
    image = apply_rows(
        rims, returned, z_ref[...], own_ref, blocks_ref, pick_ref, back_ref, picked_ref
    )
    next_ref[...] = image - SHIFT * field_ref[...]


def finish_kernel(fields, mine_ref, theirs_ref, *refs):
    value_refs = refs[: fields + 1]
    z_refs = refs[fields + 1 : 2 * fields + 1]
    solution_ref, residual_ref = refs[2 * fields + 1 :]
    total = mine_ref[...] + theirs_ref[...]
    lane = lax.broadcasted_iota(jnp.int32, (1, 128), 1)
    shape = solution_ref.shape[1:]
    width = shape[1]

    def product(at):
        return jnp.sum(jnp.where(lane == width + at, total, 0.0), axis=1, keepdims=True)

    gram = [[product(a * fields + c) for c in range(fields)] for a in range(fields)]
    last = fields - 1
    final = [gram[c + 1][last] + SHIFT * gram[c][last] for c in range(last)]
    final.append(product(fields * fields))
    gram.append([final[c] - SHIFT * gram[last][c] for c in range(fields)])
    zero = jnp.zeros((1, 1), f32)
    one = jnp.ones((1, 1), f32)

    def form(left, right):
        value = zero
        for a, left_at in enumerate(left):
            if left_at is None:
                continue
            for c, right_at in enumerate(right):
                if right_at is not None:
                    value = value + left_at * right_at * gram[a][c]
        return value

    def plus(first, second):
        if first is None:
            return second
        return first if second is None else first + second

    def scaled(scale, value):
        return None if value is None else scale * value

    residual = [one] + [None] * fields
    direction = [one] + [None] * (fields - 1)
    iterate = [None] * fields
    product_now = form(residual, direction)
    for step in range(fields):
        image = [None] * (fields + 1)
        for c in range(fields):
            if direction[c] is not None:
                image[c] = plus(image[c], SHIFT * direction[c])
                image[c + 1] = plus(image[c + 1], direction[c])
        alpha = product_now / form(image, direction)
        iterate = [plus(iterate[c], scaled(alpha, direction[c])) for c in range(fields)]
        residual = [plus(residual[a], scaled(-alpha, image[a])) for a in range(fields + 1)]
        if step + 1 < fields:
            product_next = form(residual, residual[:fields])
            beta = product_next / product_now
            direction = [plus(residual[c], scaled(beta, direction[c])) for c in range(fields)]
            product_now = product_next
    answer = iterate[0] * z_refs[0][...]
    for c in range(1, fields):
        answer = answer + iterate[c] * z_refs[c][...]
    left_over = residual[0] * value_refs[0][...].reshape(shape)
    for a in range(1, fields + 1):
        left_over = left_over + residual[a] * value_refs[a][...]
    solution_ref[0] = answer
    residual_ref[0] = left_over


def on_device(
    right_side,
    blocks,
    pattern,
    send_rows,
    inverse_blocks,
    margin_blocks,
    near_null,
    aggregate,
    coarse_inverse,
):
    rows, width = right_side.shape[1:]
    slots = blocks.shape[2]
    turns, ghosts = send_rows.shape[1:]
    extent = rows + turns * ghosts
    modes = near_null.shape[2]
    levels = lax.axis_size("sub").bit_length() - 1
    bits = [turn * levels // turns for turn in range(turns)]
    flip = [(0, 1), (1, 0)]
    row_shape = (rows, width)
    packet = (2 * ghosts, width)
    parts = rows * slots
    ghost_total = turns * ghosts
    parts_scratch = [pltpu.VMEM((parts, width), f32)]
    spread_scratch = parts_scratch + [
        pltpu.VMEM((slots, extent, width), f32),
        pltpu.SMEM((2, 128), jnp.int32),
        pltpu.SemaphoreType.DMA,
    ]
    null_view = jnp.transpose(near_null, (0, 2, 1, 3))
    pattern_view = jnp.transpose(pattern, (2, 0, 1))

    def swap(array):
        return lax.ppermute(array, "coarse", flip)

    packs = call(
        pack_kernel,
        [(ghosts, width * width // 128, 128)] * turns,
        [VMEM] + [ANY] * REPEATS,
        [margin_blocks] * (1 + REPEATS),
        name="pack_margin",
    )
    gathered = [partner(packs[turn], "sub", bits[turn]) for turn in range(turns)]
    offset, mine = call(
        restrict_kernel,
        [((rows, 128), jnp.int32), (1, 128)],
        [VMEM, VMEM, SMEM],
        [right_side, null_view, aggregate],
        name="restrict",
    )
    theirs = swap(mine)
    pick, send, back, index = call(
        table_kernel,
        [
            ((parts, 3 * extent), bf16),
            ((ghost_total, 3 * rows), bf16),
            ((rows, 3 * ghost_total), bf16),
            ((2, 128), jnp.int32),
        ],
        [SMEM, SMEM],
        [pattern_view, send_rows],
        scratch=[pltpu.VMEM((parts, 128), f32), pltpu.VMEM((ghost_total, 128), f32)],
        name="tables",
    )
    source, null_modes, held, solver = right_side, null_view, blocks, coarse_inverse
    _, row = call(
        local_kernel,
        [(rows, width, 128), row_shape],
        [VMEM, VMEM],
        [right_side, inverse_blocks],
        name="local_inverse",
    )
    base, wide = call(
        base_kernel,
        [row_shape, (width // (128 - width), ghost_total, 128)],
        [VMEM] * 8,
        [source, send, row, mine, theirs, solver, null_modes, offset],
        name="first_base",
    )
    z, own, *packets = call(
        functools.partial(first_kernel, turns),
        [row_shape, row_shape] + [packet] * turns,
        [VMEM] * (turns + 5),
        [*gathered[::-1], base, wide, back, held, index],
        scratch=spread_scratch,
        name="first_spread",
    )
    (combined,) = call(
        functools.partial(combine_kernel, turns),
        [(rows, width, width)],
        [VMEM, SMEM] + [VMEM] * turns,
        [inverse_blocks, send_rows, *gathered],
        name="combine",
    )
    values = [source]
    fields = [z]
    for step in range(ITERS - 1):
        arrived = [partner(packets[turn], "sub", bits[turn]) for turn in range(turns)]
        if step == 0:
            combined, *arrived = lax.optimization_barrier([combined, *arrived[::-1]])
            arrived = arrived[::-1]
        following, mine = call(
            functools.partial(apply_kernel, turns),
            [row_shape, (1, 128)],
            [VMEM] * (turns + 8),
            [values[-1], fields[-1], own, *arrived[::-1], held, pick, back, null_modes, offset],
            scratch=parts_scratch,
            name="apply",
        )
        values.append(following)
        theirs = swap(mine)
        column, row = call(
            local_kernel,
            [(rows, width, 128), row_shape],
            [VMEM, VMEM],
            [following, combined],
            name="local_inverse",
        )
        inputs = [column, row, mine, theirs, solver, null_modes, offset, held, index]
        if step + 2 < ITERS:
            z, own, *packets = call(
                functools.partial(spread_kernel, turns),
                [row_shape, row_shape] + [packet] * turns,
                [VMEM] * 9,
                inputs,
                scratch=spread_scratch,
                name="spread",
            )
        else:
            (early,) = call(
                functools.partial(early_dots_kernel, ITERS),
                [(1, 128)],
                [VMEM] * (2 * ITERS - 1),
                [*values, *fields],
                name="early_dots",
            )
            z, own, payload = call(
                functools.partial(last_spread_kernel, ITERS),
                [row_shape, row_shape, (lax.axis_size("sub"), 2 * ghost_total, 128)],
                [VMEM] * (10 + ITERS),
                [*inputs, early, *values],
                scratch=spread_scratch[:2]
                + [pltpu.VMEM((2 * ghost_total, 128), f32)]
                + spread_scratch[2:],
                name="last_spread",
            )
        fields.append(z)
    lines = lax.all_to_all(payload, "sub", 0, 0)
    (mine,) = call(
        functools.partial(total_kernel, bits, ITERS, width),
        [(1, 128)],
        [VMEM],
        [lines],
        name="totals",
    )
    theirs = swap(mine)
    (following,) = call(
        functools.partial(last_kernel, bits),
        [row_shape],
        [VMEM] * 7,
        [values[-1], z, own, lines, held, pick, back],
        scratch=parts_scratch,
        name="last_apply",
    )
    values.append(following)
    answer, left_over = call(
        functools.partial(finish_kernel, ITERS),
        [right_side.shape] * 2,
        [VMEM] * (2 * ITERS + 3),
        [mine, theirs, *values, *fields],
        name="finish",
    )
    return answer, left_over


def solution(mesh):
    in_specs = (
        P("coarse", "sub", None),
        P("coarse", "sub", None, None, None),
        P("coarse", "sub", None),
        P("coarse", "sub", None),
        P("coarse", "sub", None, None),
        P("coarse", "sub", None, None),
        P("coarse", "sub", None, None),
        P("coarse", "sub"),
        P("sub", None, None),
    )
    out_specs = (P("coarse", "sub", None), P("coarse", "sub", None))
    return jax.shard_map(
        on_device, mesh=mesh, in_specs=in_specs, out_specs=out_specs, check_vma=False
    )
```

```python
import functools

import jax
import jax.numpy as jnp
from jax import lax
from jax.experimental import pallas as pl
from jax.experimental.pallas import tpu as pltpu
from jax.sharding import PartitionSpec as P

ITERS = 3
SHIFT = 2.0
REPEATS = 16
LIMIT = 200.0
LARGE = 1e30

f32 = jnp.float32
bf16 = jnp.bfloat16
VMEM = pl.BlockSpec(memory_space=pltpu.VMEM)
ANY = pl.BlockSpec(memory_space=pl.ANY)
SMEM = pl.BlockSpec(memory_space=pltpu.SMEM)


def partner(array, axis, bit):
    return lax.ppermute(array, axis, [(i, i ^ 1 << bit) for i in range(lax.axis_size(axis))])


def call(kernel, outs, in_specs, args, scratch=(), name=None, cost=100000):
    return pl.pallas_call(
        kernel,
        out_shape=[
            jax.ShapeDtypeStruct(*(out if isinstance(out[0], tuple) else (out, f32))) for out in outs
        ],
        in_specs=in_specs,
        out_specs=[VMEM] * len(outs),
        scratch_shapes=list(scratch),
        compiler_params=pltpu.CompilerParams(vmem_limit_bytes=12 * 1024 * 1024),
        cost_estimate=pl.CostEstimate(flops=0, bytes_accessed=cost, transcendentals=0),
        name=name,
    )(*args)


def eye_mask(width):
    return lax.broadcasted_iota(jnp.int32, (width, width), 0) == lax.broadcasted_iota(
        jnp.int32, (width, width), 1
    )


def to_column(row, eye):
    return jnp.sum(jnp.where(eye, row, 0.0), axis=1, keepdims=True)


def to_row(column, eye):
    return jnp.sum(jnp.where(eye, column, 0.0), axis=0, keepdims=True)


def restrict(null_ref, offset_ref, field):
    offset = offset_ref[...]
    total = jnp.zeros(offset.shape, f32)
    for mode in range(null_ref.shape[1]):
        dots = jnp.sum(null_ref[0, mode] * field, axis=1, keepdims=True)
        total = total + jnp.where(offset == mode, dots, 0.0)
    return jnp.sum(total, axis=0, keepdims=True)


def coarse_field(mine_ref, theirs_ref, solver_ref, null_ref, offset_ref):
    size = solver_ref.shape[1]
    total = mine_ref[...] + theirs_ref[...]
    solved = jnp.sum(solver_ref[0] * total[:, :size], axis=1, keepdims=True)
    flat = to_row(solved, eye_mask(size))
    offset = offset_ref[:, :size]
    field = None
    for mode in range(null_ref.shape[1]):
        weight = jnp.sum(jnp.where(offset == mode, flat, 0.0), axis=1, keepdims=True)
        term = null_ref[0, mode] * weight
        field = term if field is None else field + term
    return field


def thirds(value):
    high = value.astype(bf16)
    rest = value - high.astype(f32)
    middle = rest.astype(bf16)
    low = (rest - middle.astype(f32)).astype(bf16)
    return jnp.concatenate([high, middle, low], axis=0)


def select_rows(table_ref, value):
    return jnp.dot(table_ref[...], thirds(value), preferred_element_type=f32)


def triple(table):
    return jnp.concatenate([table.astype(bf16)] * 3, axis=1)


def pack_kernel(margin_ref, *refs):
    outs = refs[REPEATS:]
    turns = len(outs)
    ghosts, _, _ = outs[0].shape
    width = margin_ref.shape[2]
    tall = width * width // 128
    side = 128 - width
    rest = width - tall
    for turn in range(turns):
        for g in range(ghosts):
            block = margin_ref[0, turn * ghosts + g]
            outs[turn][g, :, 0:width] = block[:tall]
            for piece in range(width // side):
                outs[turn][g, piece * rest : (piece + 1) * rest, width:128] = block[
                    tall:, piece * side : (piece + 1) * side
                ]


def restrict_kernel(field_ref, null_ref, aggregate_ref, offset_ref, mine_ref):
    modes = null_ref.shape[1]
    lane = lax.broadcasted_iota(jnp.int32, (1, 128), 1)
    for i in range(offset_ref.shape[0]):
        offset_ref[i : i + 1, :] = lane - aggregate_ref[0, i] * modes
    mine_ref[...] = restrict(null_ref, offset_ref, field_ref[0])


def table_kernel(
    pattern_ref, senders_ref, pick_ref, send_ref, back_ref, index_ref, table_ref, send_table_ref
):
    slots, _, rows = pattern_ref.shape
    turns, ghosts = senders_ref.shape[1:]
    extent = pick_ref.shape[1] // 3
    lane = lax.broadcasted_iota(jnp.int32, (1, 128), 1)
    columns = jnp.zeros((1, 128), jnp.int32)
    for i in range(rows):
        for j in range(slots):
            at = i * slots + j
            table_ref[at : at + 1, :] = jnp.where(lane == pattern_ref[j, 0, i], 1.0, 0.0)
            columns = jnp.where(lane == at, pattern_ref[j, 0, i], columns)
    index_ref[0:1, :] = columns
    sent = jnp.zeros((1, 128), jnp.int32)
    for turn in range(turns):
        for g in range(ghosts):
            at = turn * ghosts + g
            send_table_ref[at : at + 1, :] = jnp.where(lane == senders_ref[0, turn, g], 1.0, 0.0)
            sent = jnp.where(lane == at, senders_ref[0, turn, g], sent)
    index_ref[1:2, :] = sent
    table = table_ref[...]
    pick_ref[...] = triple(table[:, :extent])
    send_table = send_table_ref[...]
    send_ref[...] = triple(send_table[:, :rows])
    back_ref[...] = triple(send_table.T[:rows])


def load_kernel(source_ref, out_ref, *sems):
    quarter = source_ref.shape[1] // len(sems)
    copies = [
        pltpu.make_async_copy(
            source_ref.at[:, pl.ds(at * quarter, quarter)],
            out_ref.at[:, pl.ds(at * quarter, quarter)],
            sem,
        )
        for at, sem in enumerate(sems)
    ]
    for copy in copies:
        copy.start()
    for copy in copies:
        copy.wait()


def local_row_kernel(field_ref, inverse_ref, row_ref):
    rows, width = row_ref.shape
    eye = eye_mask(width)
    for i in range(rows):
        column = jnp.sum(inverse_ref[0, i] * field_ref[0, i : i + 1, :], axis=1, keepdims=True)
        row_ref[i : i + 1, :] = to_row(column, eye)


def local_kernel(field_ref, inverse_ref, column_ref, row_ref):
    rows, width = row_ref.shape
    eye = eye_mask(width)
    for i in range(rows):
        column = jnp.sum(inverse_ref[i] * field_ref[i : i + 1, :], axis=1, keepdims=True)
        column_ref[i] = jnp.broadcast_to(column, (width, 128))
        row_ref[i : i + 1, :] = to_row(column, eye)


def spread_block_row(blocks_ref, parts_ref, i, column):
    slots, width = blocks_ref.shape[2:4]
    for j in range(slots):
        part = blocks_ref[0, i, j, 0:8, :] * column[0:8]
        for start in range(8, width, 8):
            part = part + blocks_ref[0, i, j, start : start + 8, :] * column[start : start + 8]
        at = i * slots + j
        parts_ref[at : at + 1, :] = jnp.sum(part, axis=0, keepdims=True)


def scatter_rows(parts_ref, slots_ref, indices_ref, rows):
    slots = slots_ref.shape[0]
    for i in range(rows):
        slots_ref[0, i : i + 1, :] = parts_ref[i * slots : i * slots + 1, :]
        for j in range(1, slots):
            at = i * slots + j
            slots_ref[j, pl.ds(indices_ref[0, at], 1), :] = parts_ref[at : at + 1, :]
    spread = slots_ref[0]
    for j in range(1, slots):
        spread = spread + slots_ref[j]
    return spread


def finish_spread(parts_ref, slots_ref, indices_ref, z_ref, own_ref, packets):
    turns = len(packets)
    rows = z_ref.shape[0]
    ghosts = packets[0].shape[0] // 2
    spread = scatter_rows(parts_ref, slots_ref, indices_ref, rows)
    own_ref[...] = spread[:rows]
    for turn in range(turns):
        for g in range(ghosts):
            at = indices_ref[1, turn * ghosts + g]
            packets[turn][g : g + 1, :] = z_ref[pl.ds(at, 1), :]
        start = rows + turn * ghosts
        packets[turn][ghosts:, :] = spread[start : start + ghosts]


def margin_row(packed_ref, g, wide_ref, at, eye, inside):
    pieces = wide_ref.shape[0]
    tall = packed_ref.shape[1]
    rest = tall // pieces
    products = [
        packed_ref[g, piece * rest : (piece + 1) * rest, :] * wide_ref[piece, at : at + 1, :]
        for piece in range(pieces)
    ]
    beside = products[0]
    for product in products[1:]:
        beside = beside + product
    main = [jnp.where(inside, product, 0.0) for product in products]
    columns = [jnp.sum(part, axis=1, keepdims=True) for part in main]
    columns.append(jnp.sum(jnp.where(inside, 0.0, beside), axis=1, keepdims=True))
    row = None
    for piece, column in enumerate(columns):
        part = jnp.where(eye[piece * rest : (piece + 1) * rest], column, 0.0)
        row = part if row is None else row + part
    return jnp.sum(row, axis=0, keepdims=True)


def margin_rows(packed, wide_ref, eye):
    ghosts = packed[0].shape[0]
    width = eye.shape[0]
    inside = lax.broadcasted_iota(jnp.int32, (1, 128), 1) < width
    out = []
    for turn, ref in enumerate(packed):
        for g in range(ghosts):
            out.append(margin_row(ref, g, wide_ref, turn * ghosts + g, eye, inside))
    return jnp.concatenate(out, axis=0)


def base_kernel(
    field_ref,
    send_ref,
    row_ref,
    mine_ref,
    theirs_ref,
    solver_ref,
    null_ref,
    offset_ref,
    base_ref,
    wide_ref,
):
    picked = select_rows(send_ref, field_ref[0])
    width = picked.shape[1]
    side = 128 - width
    for piece in range(wide_ref.shape[0]):
        wide_ref[piece, :, :width] = picked
        wide_ref[piece, :, width:] = picked[:, piece * side : (piece + 1) * side]
    coarse = coarse_field(mine_ref, theirs_ref, solver_ref, null_ref, offset_ref)
    base_ref[...] = row_ref[...] + coarse


def combine_kernel(turns, inverse_ref, senders_ref, *refs):
    gathered = refs[:turns]
    (combined_ref,) = refs[turns:]
    ghosts, tall = gathered[0].shape[:2]
    width = inverse_ref.shape[2]
    side = 128 - width
    rest = width - tall
    combined_ref[...] = inverse_ref[0]
    for turn in range(turns):
        for g in range(ghosts):
            at = senders_ref[0, turn, g]
            combined_ref[at, 0:tall, :] += gathered[turn][g, :, 0:width]
            for piece in range(width // side):
                combined_ref[at, tall:, piece * side : (piece + 1) * side] += gathered[turn][
                    g, piece * rest : (piece + 1) * rest, width:128
                ]


def first_kernel(turns, *refs):
    packed = refs[:turns][::-1]
    base_ref, wide_ref, back_ref, blocks_ref, index_ref, z_ref, own_ref = refs[turns : turns + 7]
    packets = refs[turns + 7 : 2 * turns + 7]
    parts_ref, slots_ref, indices_ref, sem = refs[2 * turns + 7 :]
    fetch = pltpu.make_async_copy(index_ref, indices_ref, sem)
    fetch.start()
    slots_ref[...] = jnp.zeros(slots_ref.shape, f32)
    rows, width = z_ref.shape
    eye = eye_mask(width)
    margin = margin_rows(packed, wide_ref, eye)
    z = base_ref[...] + select_rows(back_ref, margin)
    z_ref[...] = z
    for i in range(rows):
        spread_block_row(blocks_ref, parts_ref, i, to_column(z[i : i + 1], eye))
    fetch.wait()
    finish_spread(parts_ref, slots_ref, indices_ref, z_ref, own_ref, packets)


def spread_rows(
    column_ref,
    row_ref,
    mine_ref,
    theirs_ref,
    solver_ref,
    null_ref,
    offset_ref,
    blocks_ref,
    z_ref,
    parts_ref,
):
    rows, width = z_ref.shape
    eye = eye_mask(width)
    coarse = coarse_field(mine_ref, theirs_ref, solver_ref, null_ref, offset_ref)
    z_ref[...] = row_ref[...] + coarse
    for i in range(rows):
        column = column_ref[i][:, :width] + to_column(coarse[i : i + 1], eye)
        spread_block_row(blocks_ref, parts_ref, i, column)


def spread_kernel(turns, *refs):
    index_ref, z_ref, own_ref = refs[8:11]
    packets = refs[11 : 11 + turns]
    parts_ref, slots_ref, indices_ref, sem = refs[11 + turns :]
    fetch = pltpu.make_async_copy(index_ref, indices_ref, sem)
    fetch.start()
    slots_ref[...] = jnp.zeros(slots_ref.shape, f32)
    spread_rows(*refs[:8], z_ref, parts_ref)
    fetch.wait()
    finish_spread(parts_ref, slots_ref, indices_ref, z_ref, own_ref, packets)


def dot_at(lane, at, first, second, packed):
    dot = jnp.sum(jnp.sum(first * second, axis=0, keepdims=True), axis=1, keepdims=True)
    return jnp.where(lane == at, dot, packed)


def early_dots_kernel(fields, *refs):
    value_refs = refs[:fields]
    z_refs = refs[fields:-1]
    rows, width = z_refs[0].shape
    lane = lax.broadcasted_iota(jnp.int32, (1, 128), 1)
    packed = jnp.zeros((1, 128), f32)
    for a in range(fields):
        value = value_refs[a][...].reshape(rows, width)
        for c, z_at in enumerate(z_refs):
            packed = dot_at(lane, width + a * fields + c, value, z_at[...], packed)
    refs[-1][...] = packed


def last_spread_kernel(fields, *refs):
    index_ref, early_ref = refs[8:10]
    value_refs = refs[10 : 10 + fields]
    z_ref, own_ref, payload_ref, parts_ref, slots_ref, line_ref, indices_ref, sem = refs[10 + fields :]
    fetch = pltpu.make_async_copy(index_ref, indices_ref, sem)
    fetch.start()
    slots_ref[...] = jnp.zeros(slots_ref.shape, f32)
    line_ref[...] = jnp.zeros(line_ref.shape, f32)
    spread_rows(*refs[:8], z_ref, parts_ref)
    rows, width = z_ref.shape
    ghosts = line_ref.shape[0] // 2
    z = z_ref[...]
    lane = lax.broadcasted_iota(jnp.int32, (1, 128), 1)
    packed = early_ref[...]
    for a in range(fields):
        value = value_refs[a][...].reshape(rows, width)
        packed = dot_at(lane, width + a * fields + fields - 1, value, z, packed)
    fetch.wait()
    spread = scatter_rows(parts_ref, slots_ref, indices_ref, rows)
    own = spread[:rows]
    own_ref[...] = own
    packed = dot_at(lane, width + fields * fields, z, own, packed)
    line_ref[0:1, :] = packed
    line_ref[0:ghosts, :width] = spread[rows:]
    for at in range(ghosts):
        line_ref[ghosts + at : ghosts + at + 1, :width] = z_ref[pl.ds(indices_ref[1, at], 1), :]
    line = line_ref[...]
    for device in range(payload_ref.shape[0]):
        payload_ref[device] = line


def total_kernel(bits, fields, width, lines_ref, out_ref):
    devices, height = lines_ref.shape[:2]
    ghosts = height // 2
    each = ghosts // len(bits)
    lane = lax.broadcasted_iota(jnp.int32, (1, 128), 1)
    packed = lines_ref[0, 0:1, :]
    for device in range(1, devices):
        packed = packed + lines_ref[device, 0:1, :]
    crossed = jnp.zeros((each, 128), f32)
    for device in range(devices):
        for turn, bit in enumerate(bits):
            start = turn * each
            crossed = crossed + (
                lines_ref[device, start : start + each, :]
                * lines_ref[device ^ (1 << bit), ghosts + start : ghosts + start + each, :]
            )
    crossed = jnp.where(lane < width, jnp.sum(crossed, axis=0, keepdims=True), 0.0)
    crossed = jnp.sum(crossed, axis=1, keepdims=True)
    at = lane == width + fields * fields
    out_ref[...] = packed + jnp.where(at, crossed, 0.0)


def apply_rows(rims, returned, z, own_ref, blocks_ref, pick_ref, back_ref, picked_ref):
    rows, width = z.shape
    slots = blocks_ref.shape[2]
    eye = eye_mask(width)
    extended = jnp.concatenate([z] + rims, axis=0)
    picked_ref[...] = select_rows(pick_ref, extended)
    returned = jnp.concatenate(returned, axis=0)
    back = own_ref[...] + select_rows(back_ref, returned)
    image = []
    for i in range(rows):
        total = None
        for j in range(slots):
            at = i * slots + j
            term = blocks_ref[0, i, j] * picked_ref[at : at + 1, :]
            total = term if total is None else total + term
        column = jnp.sum(total, axis=1, keepdims=True)
        image.append(to_row(column, eye))
    return 0.5 * (jnp.concatenate(image, axis=0) + back)


def apply_kernel(turns, field_ref, z_ref, own_ref, *refs):
    arrived = refs[:turns][::-1]
    (
        blocks_ref,
        pick_ref,
        back_ref,
        null_ref,
        offset_ref,
        next_ref,
        coarse_ref,
        picked_ref,
    ) = refs[turns:]
    ghosts = arrived[0].shape[0] // 2
    rims = [ref[0:ghosts, :] for ref in arrived]
    returned = [ref[ghosts:, :] for ref in arrived]
    image = apply_rows(
        rims, returned, z_ref[...], own_ref, blocks_ref, pick_ref, back_ref, picked_ref
    )
    following = image - SHIFT * field_ref[...].reshape(image.shape)
    next_ref[...] = following
    coarse_ref[...] = restrict(null_ref, offset_ref, following)


def last_kernel(
    bits,
    field_ref,
    z_ref,
    own_ref,
    lines_ref,
    blocks_ref,
    pick_ref,
    back_ref,
    next_ref,
    picked_ref,
):
    width = z_ref.shape[1]
    ghosts = lines_ref.shape[1] // 2
    each = ghosts // len(bits)
    here = lax.axis_index("sub")
    rims = []
    returned = []
    for turn, bit in enumerate(bits):
        start = turn * each
        there = jnp.bitwise_xor(here, 1 << bit)
        returned.append(lines_ref[there, start : start + each, :width])
        rims.append(lines_ref[there, ghosts + start : ghosts + start + each, :width])
    image = apply_rows(
        rims, returned, z_ref[...], own_ref, blocks_ref, pick_ref, back_ref, picked_ref
    )
    next_ref[...] = image - SHIFT * field_ref[...]


def coefficients(total, fields, width):
    lane = lax.broadcasted_iota(jnp.int32, (1, 128), 1)

    def product(at):
        return jnp.sum(jnp.where(lane == width + at, total, 0.0), axis=1, keepdims=True)

    gram = [[product(a * fields + c) for c in range(fields)] for a in range(fields)]
    last = fields - 1
    final = [gram[c + 1][last] + SHIFT * gram[c][last] for c in range(last)]
    final.append(product(fields * fields))
    gram.append([final[c] - SHIFT * gram[last][c] for c in range(fields)])
    one = jnp.ones((1, 1), f32)
    checks = []

    def form(left, right):
        value = jnp.zeros((1, 1), f32)
        size = jnp.zeros((1, 1), f32)
        for a, left_at in enumerate(left):
            if left_at is None:
                continue
            for c, right_at in enumerate(right):
                if right_at is not None:
                    term = left_at * right_at * gram[a][c]
                    value = value + term
                    size = size + jnp.abs(term)
        checks.append((size <= LIMIT * jnp.abs(value)) & (size < LARGE) & (size > 1.0 / LARGE))
        return value

    def plus(first, second):
        if first is None:
            return second
        return first if second is None else first + second

    def scaled(scale, value):
        return None if value is None else scale * value

    residual = [one] + [None] * fields
    direction = [one] + [None] * (fields - 1)
    iterate = [None] * fields
    product_now = form(residual, direction)
    for step in range(fields):
        image = [None] * (fields + 1)
        for c in range(fields):
            if direction[c] is not None:
                image[c] = plus(image[c], SHIFT * direction[c])
                image[c + 1] = plus(image[c + 1], direction[c])
        alpha = product_now / form(image, direction)
        iterate = [plus(iterate[c], scaled(alpha, direction[c])) for c in range(fields)]
        residual = [plus(residual[a], scaled(-alpha, image[a])) for a in range(fields + 1)]
        if step + 1 < fields:
            product_next = form(residual, residual[:fields])
            beta = product_next / product_now
            direction = [plus(residual[c], scaled(beta, direction[c])) for c in range(fields)]
            product_now = product_next
    sound = checks[0]
    for check in checks[1:]:
        sound = sound & check
    return iterate, residual, sound


def decide_kernel(fields, width, mine_ref, theirs_ref, out_ref):
    _, _, sound = coefficients(mine_ref[...] + theirs_ref[...], fields, width)
    out_ref[...] = jnp.broadcast_to(jnp.where(sound, 1.0, 0.0), out_ref.shape)


def finish_kernel(fields, mine_ref, theirs_ref, *refs):
    value_refs = refs[: fields + 1]
    z_refs = refs[fields + 1 : 2 * fields + 1]
    solution_ref, residual_ref = refs[2 * fields + 1 :]
    shape = solution_ref.shape[1:]
    iterate, residual, _ = coefficients(mine_ref[...] + theirs_ref[...], fields, shape[1])
    answer = iterate[0] * z_refs[0][...]
    for c in range(1, fields):
        answer = answer + iterate[c] * z_refs[c][...]
    left_over = residual[0] * value_refs[0][...].reshape(shape)
    for a in range(1, fields + 1):
        left_over = left_over + residual[a] * value_refs[a][...]
    solution_ref[0] = answer
    residual_ref[0] = left_over


def step_by_step(bits, source, matrix, columns, senders, inverse, null_modes, groups_of, coarse_inv):
    highest = lax.Precision.HIGHEST
    row_count, width = source.shape
    turns, ghost_count = senders.shape
    extent = row_count + turns * ghost_count
    mode_count = null_modes.shape[1]
    group_count = coarse_inv.shape[0] // mode_count

    def table(size, index):
        return (jnp.arange(size, dtype=jnp.int32)[:, None] == index[None, :]).astype(f32)

    column_table = table(extent, columns.reshape(-1))
    sender_table = table(row_count, senders.reshape(-1))
    group_table = table(group_count, groups_of)

    def precondition(residual):
        local = jnp.einsum("rmb,rb->rm", null_modes, residual, precision=highest)
        total = lax.psum(jnp.dot(group_table, local, precision=highest), "coarse")
        solved = jnp.dot(coarse_inv, total.reshape(-1), precision=highest)
        per_row = jnp.dot(
            group_table.T, solved.reshape(group_count, mode_count), precision=highest
        )
        coarse = jnp.einsum("rmb,rm->rb", null_modes, per_row, precision=highest)
        return jnp.einsum("rab,rb->ra", inverse, residual, precision=highest) + coarse

    def operate(field):
        transposed = jnp.einsum("rkab,ra->rkb", matrix, field, precision=highest)
        spread = jnp.dot(column_table, transposed.reshape(-1, width), precision=highest)
        sent = jnp.dot(sender_table.T, field, precision=highest)
        rims = []
        returned = []
        for turn in range(turns):
            start = turn * ghost_count
            packet = jnp.concatenate(
                [
                    sent[start : start + ghost_count],
                    spread[row_count + start : row_count + start + ghost_count],
                ],
                axis=0,
            )
            arrived = partner(packet, "sub", bits[turn])
            rims.append(arrived[:ghost_count])
            returned.append(arrived[ghost_count:])
        extended = jnp.concatenate([field] + rims, axis=0)
        picked = jnp.dot(column_table.T, extended, precision=highest)
        picked = picked.reshape(row_count, -1, width)
        forward = jnp.einsum("rkab,rkb->ra", matrix, picked, precision=highest)
        back = jnp.dot(sender_table, jnp.concatenate(returned, axis=0), precision=highest)
        return 0.5 * (forward + (spread[:row_count] + back))

    def everywhere(first, second):
        return lax.psum(jnp.sum(first * second), ("sub", "coarse"))

    def body(step, state):
        answer, residual, direction, product_now = state
        precond = precondition(residual)
        product_next = everywhere(residual, precond)
        ratio = jnp.where(step == 0, 0.0, product_next / product_now)
        direction = precond + ratio * direction
        image = operate(direction)
        alpha = product_next / everywhere(direction, image)
        return (answer + alpha * direction, residual - alpha * image, direction, product_next)

    zeros = jnp.zeros_like(source)
    answer, residual, _, _ = lax.fori_loop(
        0, ITERS, body, (zeros, source, zeros, jnp.ones((), f32))
    )
    return answer[None], residual[None]


def on_device(
    right_side,
    blocks,
    pattern,
    send_rows,
    inverse_blocks,
    margin_blocks,
    near_null,
    aggregate,
    coarse_inverse,
):
    rows, width = right_side.shape[1:]
    slots = blocks.shape[2]
    turns, ghosts = send_rows.shape[1:]
    extent = rows + turns * ghosts
    modes = near_null.shape[2]
    levels = lax.axis_size("sub").bit_length() - 1
    bits = [turn * levels // turns for turn in range(turns)]
    flip = [(0, 1), (1, 0)]
    row_shape = (rows, width)
    packet = (2 * ghosts, width)
    parts = rows * slots
    ghost_total = turns * ghosts
    parts_scratch = [pltpu.VMEM((parts, width), f32)]
    spread_scratch = parts_scratch + [
        pltpu.VMEM((slots, extent, width), f32),
        pltpu.SMEM((2, 128), jnp.int32),
        pltpu.SemaphoreType.DMA,
    ]
    null_view = jnp.transpose(near_null, (0, 2, 1, 3))
    pattern_view = jnp.transpose(pattern, (2, 0, 1))

    def swap(array):
        return lax.ppermute(array, "coarse", flip)

    packs = call(
        pack_kernel,
        [(ghosts, width * width // 128, 128)] * turns,
        [VMEM] + [ANY] * REPEATS,
        [margin_blocks] * (1 + REPEATS),
        name="pack_margin",
    )
    gathered = [partner(packs[turn], "sub", bits[turn]) for turn in range(turns)]
    offset, mine = call(
        restrict_kernel,
        [((rows, 128), jnp.int32), (1, 128)],
        [VMEM, VMEM, SMEM],
        [right_side, null_view, aggregate],
        name="restrict",
    )
    theirs = swap(mine)
    pick, send, back, index = call(
        table_kernel,
        [
            ((parts, 3 * extent), bf16),
            ((ghost_total, 3 * rows), bf16),
            ((rows, 3 * ghost_total), bf16),
            ((2, 128), jnp.int32),
        ],
        [SMEM, SMEM],
        [pattern_view, send_rows],
        scratch=[pltpu.VMEM((parts, 128), f32), pltpu.VMEM((ghost_total, 128), f32)],
        name="tables",
    )
    source, null_modes, solver = right_side, null_view, coarse_inverse
    (held,) = call(
        load_kernel,
        [blocks.shape],
        [ANY],
        [blocks],
        scratch=[pltpu.SemaphoreType.DMA] * 4,
        name="load_blocks",
        cost=8000000,
    )
    (row,) = call(
        local_row_kernel,
        [row_shape],
        [VMEM, VMEM],
        [right_side, inverse_blocks],
        name="local_rows",
    )
    base, wide = call(
        base_kernel,
        [row_shape, (width // (128 - width), ghost_total, 128)],
        [VMEM] * 8,
        [source, send, row, mine, theirs, solver, null_modes, offset],
        name="first_base",
    )
    z, own, *packets = call(
        functools.partial(first_kernel, turns),
        [row_shape, row_shape] + [packet] * turns,
        [VMEM] * (turns + 5),
        [*gathered[::-1], base, wide, back, held, index],
        scratch=spread_scratch,
        name="first_spread",
    )
    (combined,) = call(
        functools.partial(combine_kernel, turns),
        [(rows, width, width)],
        [VMEM, SMEM] + [VMEM] * turns,
        [inverse_blocks, send_rows, *gathered],
        name="combine",
    )
    values = [source]
    fields = [z]
    for step in range(ITERS - 1):
        arrived = [partner(packets[turn], "sub", bits[turn]) for turn in range(turns)]
        if step == 0:
            combined, *arrived = lax.optimization_barrier([combined, *arrived[::-1]])
            arrived = arrived[::-1]
        following, mine = call(
            functools.partial(apply_kernel, turns),
            [row_shape, (1, 128)],
            [VMEM] * (turns + 8),
            [values[-1], fields[-1], own, *arrived[::-1], held, pick, back, null_modes, offset],
            scratch=parts_scratch,
            name="apply",
        )
        values.append(following)
        theirs = swap(mine)
        column, row = call(
            local_kernel,
            [(rows, width, 128), row_shape],
            [VMEM, VMEM],
            [following, combined],
            name="local_inverse",
        )
        inputs = [column, row, mine, theirs, solver, null_modes, offset, held, index]
        if step + 2 < ITERS:
            z, own, *packets = call(
                functools.partial(spread_kernel, turns),
                [row_shape, row_shape] + [packet] * turns,
                [VMEM] * 9,
                inputs,
                scratch=spread_scratch,
                name="spread",
            )
        else:
            (early,) = call(
                functools.partial(early_dots_kernel, ITERS),
                [(1, 128)],
                [VMEM] * (2 * ITERS - 1),
                [*values, *fields],
                name="early_dots",
            )
            z, own, payload = call(
                functools.partial(last_spread_kernel, ITERS),
                [row_shape, row_shape, (lax.axis_size("sub"), 2 * ghost_total, 128)],
                [VMEM] * (10 + ITERS),
                [*inputs, early, *values],
                scratch=spread_scratch[:2]
                + [pltpu.VMEM((2 * ghost_total, 128), f32)]
                + spread_scratch[2:],
                name="last_spread",
            )
        fields.append(z)
    lines = lax.all_to_all(payload, "sub", 0, 0)
    (mine,) = call(
        functools.partial(total_kernel, bits, ITERS, width),
        [(1, 128)],
        [VMEM],
        [lines],
        name="totals",
    )
    theirs = swap(mine)
    (following,) = call(
        functools.partial(last_kernel, bits),
        [row_shape],
        [VMEM] * 7,
        [values[-1], z, own, lines, held, pick, back],
        scratch=parts_scratch,
        name="last_apply",
    )
    values.append(following)
    (sound,) = call(
        functools.partial(decide_kernel, ITERS, width),
        [(1, 128)],
        [VMEM, VMEM],
        [mine, theirs],
        name="decide",
    )

    def finish():
        return tuple(
            call(
                functools.partial(finish_kernel, ITERS),
                [right_side.shape] * 2,
                [VMEM] * (2 * ITERS + 3),
                [mine, theirs, *values, *fields],
                name="finish",
            )
        )

    def again():
        nought = sound[0, 0]
        whole = nought.astype(jnp.int32)
        return step_by_step(
            bits,
            right_side[0] + nought,
            blocks[0] + nought,
            pattern[0] + whole,
            send_rows[0] + whole,
            combined + nought,
            near_null[0] + nought,
            aggregate[0] + whole,
            coarse_inverse[0] + nought,
        )

    return lax.cond(sound[0, 0] > 0.5, finish, again)


def solution(mesh):
    in_specs = (
        P("coarse", "sub", None),
        P("coarse", "sub", None, None, None),
        P("coarse", "sub", None),
        P("coarse", "sub", None),
        P("coarse", "sub", None, None),
        P("coarse", "sub", None, None),
        P("coarse", "sub", None, None),
        P("coarse", "sub"),
        P("sub", None, None),
    )
    out_specs = (P("coarse", "sub", None), P("coarse", "sub", None))
    return jax.shard_map(
        on_device, mesh=mesh, in_specs=in_specs, out_specs=out_specs, check_vma=False
    )
```

```python
import functools

import jax
import jax.numpy as jnp
from jax import lax
from jax.experimental import pallas as pl
from jax.experimental.pallas import tpu as pltpu
from jax.sharding import PartitionSpec as P

ITERS = 3
SHIFT = 2.0
REPEATS = 16
LIMIT = 200.0
LARGE = 1e30

f32 = jnp.float32
bf16 = jnp.bfloat16
VMEM = pl.BlockSpec(memory_space=pltpu.VMEM)
ANY = pl.BlockSpec(memory_space=pl.ANY)
SMEM = pl.BlockSpec(memory_space=pltpu.SMEM)


def partner(array, axis, bit):
    return lax.ppermute(array, axis, [(i, i ^ 1 << bit) for i in range(lax.axis_size(axis))])


def call(kernel, outs, in_specs, args, scratch=(), name=None, cost=100000):
    return pl.pallas_call(
        kernel,
        out_shape=[
            jax.ShapeDtypeStruct(*(out if isinstance(out[0], tuple) else (out, f32))) for out in outs
        ],
        in_specs=in_specs,
        out_specs=[VMEM] * len(outs),
        scratch_shapes=list(scratch),
        compiler_params=pltpu.CompilerParams(vmem_limit_bytes=12 * 1024 * 1024),
        cost_estimate=pl.CostEstimate(flops=0, bytes_accessed=cost, transcendentals=0),
        name=name,
    )(*args)


def eye_mask(width):
    return lax.broadcasted_iota(jnp.int32, (width, width), 0) == lax.broadcasted_iota(
        jnp.int32, (width, width), 1
    )


def to_column(row, eye):
    return jnp.sum(jnp.where(eye, row, 0.0), axis=1, keepdims=True)


def to_row(column, eye):
    return jnp.sum(jnp.where(eye, column, 0.0), axis=0, keepdims=True)


def restrict(null_ref, offset_ref, field):
    offset = offset_ref[...]
    total = jnp.zeros(offset.shape, f32)
    for mode in range(null_ref.shape[1]):
        dots = jnp.sum(null_ref[0, mode] * field, axis=1, keepdims=True)
        total = total + jnp.where(offset == mode, dots, 0.0)
    return jnp.sum(total, axis=0, keepdims=True)


def coarse_solve(mine_ref, theirs_ref, solver_ref):
    size = solver_ref.shape[1]
    total = mine_ref[...] + theirs_ref[...]
    solved = jnp.sum(solver_ref[0] * total[:, :size], axis=1, keepdims=True)
    return to_row(solved, eye_mask(size))


def coarse_combine(flat, offset, terms):
    offset = offset[:, : flat.shape[1]]
    field = None
    for mode, term in enumerate(terms):
        weight = jnp.sum(jnp.where(offset == mode, flat, 0.0), axis=1, keepdims=True)
        field = term * weight if field is None else field + term * weight
    return field


def coarse_field(mine_ref, theirs_ref, solver_ref, null_ref, offset_ref):
    flat = coarse_solve(mine_ref, theirs_ref, solver_ref)
    terms = [null_ref[0, mode] for mode in range(null_ref.shape[1])]
    return coarse_combine(flat, offset_ref[...], terms)


def thirds(value):
    high = value.astype(bf16)
    rest = value - high.astype(f32)
    middle = rest.astype(bf16)
    low = (rest - middle.astype(f32)).astype(bf16)
    return jnp.concatenate([high, middle, low], axis=0)


def select_rows(table_ref, value):
    return jnp.dot(table_ref[...], thirds(value), preferred_element_type=f32)


def triple(table):
    return jnp.concatenate([table.astype(bf16)] * 3, axis=1)


def pack_kernel(margin_ref, *refs):
    outs = refs[REPEATS:]
    turns = len(outs)
    ghosts, _, _ = outs[0].shape
    width = margin_ref.shape[2]
    tall = width * width // 128
    side = 128 - width
    rest = width - tall
    for turn in range(turns):
        for g in range(ghosts):
            block = margin_ref[0, turn * ghosts + g]
            outs[turn][g, :, 0:width] = block[:tall]
            for piece in range(width // side):
                outs[turn][g, piece * rest : (piece + 1) * rest, width:128] = block[
                    tall:, piece * side : (piece + 1) * side
                ]


def restrict_kernel(field_ref, null_ref, aggregate_ref, offset_ref, wide_offset_ref, mine_ref):
    modes = null_ref.shape[1]
    lane = lax.broadcasted_iota(jnp.int32, (1, 128), 1)
    for i in range(offset_ref.shape[0]):
        offset = lane - aggregate_ref[0, i] * modes
        offset_ref[i : i + 1, :] = offset
        each = wide_offset_ref.shape[0] // offset_ref.shape[0]
        wide_offset_ref[i * each : (i + 1) * each, :] = jnp.broadcast_to(offset, (each, 128))
    mine_ref[...] = restrict(null_ref, offset_ref, field_ref[0])


def table_kernel(
    pattern_ref, senders_ref, pick_ref, send_ref, back_ref, index_ref, table_ref, send_table_ref
):
    slots, _, rows = pattern_ref.shape
    turns, ghosts = senders_ref.shape[1:]
    extent = pick_ref.shape[1] // 3
    lane = lax.broadcasted_iota(jnp.int32, (1, 128), 1)
    columns = jnp.zeros((1, 128), jnp.int32)
    for i in range(rows):
        for j in range(slots):
            at = i * slots + j
            table_ref[at : at + 1, :] = jnp.where(lane == pattern_ref[j, 0, i], 1.0, 0.0)
            columns = jnp.where(lane == at, pattern_ref[j, 0, i], columns)
    index_ref[0:1, :] = columns
    sent = jnp.zeros((1, 128), jnp.int32)
    for turn in range(turns):
        for g in range(ghosts):
            at = turn * ghosts + g
            send_table_ref[at : at + 1, :] = jnp.where(lane == senders_ref[0, turn, g], 1.0, 0.0)
            sent = jnp.where(lane == at, senders_ref[0, turn, g], sent)
    index_ref[1:2, :] = sent
    table = table_ref[...]
    pick_ref[...] = triple(table[:, :extent])
    send_table = send_table_ref[...]
    send_ref[...] = triple(send_table[:, :rows])
    back_ref[...] = triple(send_table.T[:rows])


def load_kernel(source_ref, out_ref, *sems):
    quarter = source_ref.shape[1] // len(sems)
    copies = [
        pltpu.make_async_copy(
            source_ref.at[:, pl.ds(at * quarter, quarter)],
            out_ref.at[:, pl.ds(at * quarter, quarter)],
            sem,
        )
        for at, sem in enumerate(sems)
    ]
    for copy in copies:
        copy.start()
    for copy in copies:
        copy.wait()


def local_row_kernel(field_ref, inverse_ref, row_ref):
    rows, width = row_ref.shape
    eye = eye_mask(width)
    for i in range(rows):
        column = jnp.sum(inverse_ref[0, i] * field_ref[0, i : i + 1, :], axis=1, keepdims=True)
        row_ref[i : i + 1, :] = to_row(column, eye)


def local_kernel(field_ref, inverse_ref, blocks_ref, row_ref, parts_ref):
    rows, width = row_ref.shape
    eye = eye_mask(width)
    for i in range(rows):
        column = jnp.sum(inverse_ref[i] * field_ref[i : i + 1, :], axis=1, keepdims=True)
        row_ref[i : i + 1, :] = to_row(column, eye)
        spread_block_row(blocks_ref, parts_ref, i, column)


def modes_kernel(first, blocks_ref, null_ref, out_ref):
    rows, width = null_ref.shape[2:]
    modes = out_ref.shape[0]
    slots = blocks_ref.shape[2]
    eye = eye_mask(width)

    def body(i, carry):
        columns = [
            to_column(null_ref[0, first + mode, pl.ds(i, 1), :], eye) for mode in range(modes)
        ]
        for j in range(slots):
            sums = [None] * modes
            for start in range(0, width, 8):
                tile = blocks_ref[0, i, j, start : start + 8, :]
                for mode in range(modes):
                    term = tile * columns[mode][start : start + 8]
                    sums[mode] = term if start == 0 else sums[mode] + term
            for mode in range(modes):
                out_ref[mode, pl.ds(i * slots + j, 1), :] = jnp.sum(
                    sums[mode], axis=0, keepdims=True
                )
        return carry

    lax.fori_loop(0, rows, body, 0, unroll=2)


def spread_block_row(blocks_ref, parts_ref, i, column):
    slots, width = blocks_ref.shape[2:4]
    for j in range(slots):
        part = blocks_ref[0, i, j, 0:8, :] * column[0:8]
        for start in range(8, width, 8):
            part = part + blocks_ref[0, i, j, start : start + 8, :] * column[start : start + 8]
        at = i * slots + j
        parts_ref[at : at + 1, :] = jnp.sum(part, axis=0, keepdims=True)


def scatter_rows(parts_ref, slots_ref, indices_ref, rows):
    slots = slots_ref.shape[0]
    for i in range(rows):
        slots_ref[0, i : i + 1, :] = parts_ref[i * slots : i * slots + 1, :]
        for j in range(1, slots):
            at = i * slots + j
            slots_ref[j, pl.ds(indices_ref[0, at], 1), :] = parts_ref[at : at + 1, :]
    spread = slots_ref[0]
    for j in range(1, slots):
        spread = spread + slots_ref[j]
    return spread


def finish_spread(parts_ref, slots_ref, indices_ref, z_ref, own_ref, packets):
    turns = len(packets)
    rows = z_ref.shape[0]
    ghosts = packets[0].shape[0] // 2
    spread = scatter_rows(parts_ref, slots_ref, indices_ref, rows)
    own_ref[...] = spread[:rows]
    for turn in range(turns):
        for g in range(ghosts):
            at = indices_ref[1, turn * ghosts + g]
            packets[turn][g : g + 1, :] = z_ref[pl.ds(at, 1), :]
        start = rows + turn * ghosts
        packets[turn][ghosts:, :] = spread[start : start + ghosts]


def margin_row(packed_ref, g, wide_ref, at, eye, inside):
    pieces = wide_ref.shape[0]
    tall = packed_ref.shape[1]
    rest = tall // pieces
    products = [
        packed_ref[g, piece * rest : (piece + 1) * rest, :] * wide_ref[piece, at : at + 1, :]
        for piece in range(pieces)
    ]
    beside = products[0]
    for product in products[1:]:
        beside = beside + product
    main = [jnp.where(inside, product, 0.0) for product in products]
    columns = [jnp.sum(part, axis=1, keepdims=True) for part in main]
    columns.append(jnp.sum(jnp.where(inside, 0.0, beside), axis=1, keepdims=True))
    row = None
    for piece, column in enumerate(columns):
        part = jnp.where(eye[piece * rest : (piece + 1) * rest], column, 0.0)
        row = part if row is None else row + part
    return jnp.sum(row, axis=0, keepdims=True)


def margin_rows(packed, wide_ref, eye):
    ghosts = packed[0].shape[0]
    width = eye.shape[0]
    inside = lax.broadcasted_iota(jnp.int32, (1, 128), 1) < width
    out = []
    for turn, ref in enumerate(packed):
        for g in range(ghosts):
            out.append(margin_row(ref, g, wide_ref, turn * ghosts + g, eye, inside))
    return jnp.concatenate(out, axis=0)


def base_kernel(
    field_ref,
    send_ref,
    row_ref,
    mine_ref,
    theirs_ref,
    solver_ref,
    null_ref,
    offset_ref,
    base_ref,
    wide_ref,
):
    picked = select_rows(send_ref, field_ref[0])
    width = picked.shape[1]
    side = 128 - width
    for piece in range(wide_ref.shape[0]):
        wide_ref[piece, :, :width] = picked
        wide_ref[piece, :, width:] = picked[:, piece * side : (piece + 1) * side]
    coarse = coarse_field(mine_ref, theirs_ref, solver_ref, null_ref, offset_ref)
    base_ref[...] = row_ref[...] + coarse


def combine_kernel(turns, inverse_ref, senders_ref, *refs):
    gathered = refs[:turns]
    (combined_ref,) = refs[turns:]
    ghosts, tall = gathered[0].shape[:2]
    width = inverse_ref.shape[2]
    side = 128 - width
    rest = width - tall
    combined_ref[...] = inverse_ref[0]
    for turn in range(turns):
        for g in range(ghosts):
            at = senders_ref[0, turn, g]
            combined_ref[at, 0:tall, :] += gathered[turn][g, :, 0:width]
            for piece in range(width // side):
                combined_ref[at, tall:, piece * side : (piece + 1) * side] += gathered[turn][
                    g, piece * rest : (piece + 1) * rest, width:128
                ]


def first_kernel(turns, *refs):
    packed = refs[:turns][::-1]
    base_ref, wide_ref, back_ref, blocks_ref, index_ref, z_ref, own_ref = refs[turns : turns + 7]
    packets = refs[turns + 7 : 2 * turns + 7]
    parts_ref, slots_ref, indices_ref, sem = refs[2 * turns + 7 :]
    fetch = pltpu.make_async_copy(index_ref, indices_ref, sem)
    fetch.start()
    slots_ref[...] = jnp.zeros(slots_ref.shape, f32)
    rows, width = z_ref.shape
    eye = eye_mask(width)
    margin = margin_rows(packed, wide_ref, eye)
    z = base_ref[...] + select_rows(back_ref, margin)
    z_ref[...] = z
    for i in range(rows):
        spread_block_row(blocks_ref, parts_ref, i, to_column(z[i : i + 1], eye))
    fetch.wait()
    finish_spread(parts_ref, slots_ref, indices_ref, z_ref, own_ref, packets)


def spread_rows(
    local_ref,
    row_ref,
    mine_ref,
    theirs_ref,
    solver_ref,
    null_ref,
    offset_ref,
    wide_offset_ref,
    early_modes_ref,
    late_modes_ref,
    z_ref,
    parts_ref,
):
    flat = coarse_solve(mine_ref, theirs_ref, solver_ref)
    modes = null_ref.shape[1]
    terms = [ref[mode] for ref in (early_modes_ref, late_modes_ref) for mode in range(ref.shape[0])]
    added = coarse_combine(flat, wide_offset_ref[...], terms)
    parts_ref[...] = local_ref[...] + added
    coarse = coarse_combine(flat, offset_ref[...], [null_ref[0, mode] for mode in range(modes)])
    z_ref[...] = row_ref[...] + coarse


def spread_kernel(turns, *refs):
    index_ref, z_ref, own_ref = refs[10:13]
    packets = refs[13 : 13 + turns]
    parts_ref, slots_ref, indices_ref, sem = refs[13 + turns :]
    fetch = pltpu.make_async_copy(index_ref, indices_ref, sem)
    fetch.start()
    slots_ref[...] = jnp.zeros(slots_ref.shape, f32)
    spread_rows(*refs[:10], z_ref, parts_ref)
    fetch.wait()
    finish_spread(parts_ref, slots_ref, indices_ref, z_ref, own_ref, packets)


def dot_at(lane, at, first, second, packed):
    dot = jnp.sum(jnp.sum(first * second, axis=0, keepdims=True), axis=1, keepdims=True)
    return jnp.where(lane == at, dot, packed)


def early_dots_kernel(fields, *refs):
    value_refs = refs[:fields]
    z_refs = refs[fields:-1]
    rows, width = z_refs[0].shape
    lane = lax.broadcasted_iota(jnp.int32, (1, 128), 1)
    packed = jnp.zeros((1, 128), f32)
    for a in range(fields):
        value = value_refs[a][...].reshape(rows, width)
        for c, z_at in enumerate(z_refs):
            packed = dot_at(lane, width + a * fields + c, value, z_at[...], packed)
    refs[-1][...] = packed


def last_spread_kernel(fields, *refs):
    index_ref, early_ref = refs[10:12]
    value_refs = refs[12 : 12 + fields]
    z_ref, own_ref, payload_ref, parts_ref, slots_ref, line_ref, indices_ref, sem = refs[12 + fields :]
    fetch = pltpu.make_async_copy(index_ref, indices_ref, sem)
    fetch.start()
    slots_ref[...] = jnp.zeros(slots_ref.shape, f32)
    line_ref[...] = jnp.zeros(line_ref.shape, f32)
    spread_rows(*refs[:10], z_ref, parts_ref)
    rows, width = z_ref.shape
    ghosts = line_ref.shape[0] // 2
    z = z_ref[...]
    lane = lax.broadcasted_iota(jnp.int32, (1, 128), 1)
    packed = early_ref[...]
    for a in range(fields):
        value = value_refs[a][...].reshape(rows, width)
        packed = dot_at(lane, width + a * fields + fields - 1, value, z, packed)
    fetch.wait()
    spread = scatter_rows(parts_ref, slots_ref, indices_ref, rows)
    own = spread[:rows]
    own_ref[...] = own
    packed = dot_at(lane, width + fields * fields, z, own, packed)
    line_ref[0:1, :] = packed
    line_ref[0:ghosts, :width] = spread[rows:]
    for at in range(ghosts):
        line_ref[ghosts + at : ghosts + at + 1, :width] = z_ref[pl.ds(indices_ref[1, at], 1), :]
    line = line_ref[...]
    for device in range(payload_ref.shape[0]):
        payload_ref[device] = line


def total_kernel(bits, fields, width, lines_ref, out_ref):
    devices, height = lines_ref.shape[:2]
    ghosts = height // 2
    each = ghosts // len(bits)
    lane = lax.broadcasted_iota(jnp.int32, (1, 128), 1)
    packed = lines_ref[0, 0:1, :]
    for device in range(1, devices):
        packed = packed + lines_ref[device, 0:1, :]
    crossed = jnp.zeros((each, 128), f32)
    for device in range(devices):
        for turn, bit in enumerate(bits):
            start = turn * each
            crossed = crossed + (
                lines_ref[device, start : start + each, :]
                * lines_ref[device ^ (1 << bit), ghosts + start : ghosts + start + each, :]
            )
    crossed = jnp.where(lane < width, jnp.sum(crossed, axis=0, keepdims=True), 0.0)
    crossed = jnp.sum(crossed, axis=1, keepdims=True)
    at = lane == width + fields * fields
    out_ref[...] = packed + jnp.where(at, crossed, 0.0)


def apply_rows(rims, returned, z, own_ref, blocks_ref, pick_ref, back_ref, picked_ref):
    rows, width = z.shape
    slots = blocks_ref.shape[2]
    eye = eye_mask(width)
    extended = jnp.concatenate([z] + rims, axis=0)
    picked_ref[...] = select_rows(pick_ref, extended)
    returned = jnp.concatenate(returned, axis=0)
    back = own_ref[...] + select_rows(back_ref, returned)
    image = []
    for i in range(rows):
        total = None
        for j in range(slots):
            at = i * slots + j
            term = blocks_ref[0, i, j] * picked_ref[at : at + 1, :]
            total = term if total is None else total + term
        column = jnp.sum(total, axis=1, keepdims=True)
        image.append(to_row(column, eye))
    return 0.5 * (jnp.concatenate(image, axis=0) + back)


def apply_kernel(turns, field_ref, z_ref, own_ref, *refs):
    arrived = refs[:turns][::-1]
    (
        blocks_ref,
        pick_ref,
        back_ref,
        null_ref,
        offset_ref,
        next_ref,
        coarse_ref,
        picked_ref,
    ) = refs[turns:]
    ghosts = arrived[0].shape[0] // 2
    rims = [ref[0:ghosts, :] for ref in arrived]
    returned = [ref[ghosts:, :] for ref in arrived]
    image = apply_rows(
        rims, returned, z_ref[...], own_ref, blocks_ref, pick_ref, back_ref, picked_ref
    )
    following = image - SHIFT * field_ref[...].reshape(image.shape)
    next_ref[...] = following
    coarse_ref[...] = restrict(null_ref, offset_ref, following)


def last_kernel(
    bits,
    field_ref,
    z_ref,
    own_ref,
    lines_ref,
    blocks_ref,
    pick_ref,
    back_ref,
    next_ref,
    picked_ref,
):
    width = z_ref.shape[1]
    ghosts = lines_ref.shape[1] // 2
    each = ghosts // len(bits)
    here = lax.axis_index("sub")
    rims = []
    returned = []
    for turn, bit in enumerate(bits):
        start = turn * each
        there = jnp.bitwise_xor(here, 1 << bit)
        returned.append(lines_ref[there, start : start + each, :width])
        rims.append(lines_ref[there, ghosts + start : ghosts + start + each, :width])
    image = apply_rows(
        rims, returned, z_ref[...], own_ref, blocks_ref, pick_ref, back_ref, picked_ref
    )
    next_ref[...] = image - SHIFT * field_ref[...]


def coefficients(total, fields, width):
    lane = lax.broadcasted_iota(jnp.int32, (1, 128), 1)

    def product(at):
        return jnp.sum(jnp.where(lane == width + at, total, 0.0), axis=1, keepdims=True)

    gram = [[product(a * fields + c) for c in range(fields)] for a in range(fields)]
    last = fields - 1
    final = [gram[c + 1][last] + SHIFT * gram[c][last] for c in range(last)]
    final.append(product(fields * fields))
    gram.append([final[c] - SHIFT * gram[last][c] for c in range(fields)])
    one = jnp.ones((1, 1), f32)
    checks = []

    def form(left, right):
        value = jnp.zeros((1, 1), f32)
        size = jnp.zeros((1, 1), f32)
        for a, left_at in enumerate(left):
            if left_at is None:
                continue
            for c, right_at in enumerate(right):
                if right_at is not None:
                    term = left_at * right_at * gram[a][c]
                    value = value + term
                    size = size + jnp.abs(term)
        checks.append((size <= LIMIT * jnp.abs(value)) & (size < LARGE) & (size > 1.0 / LARGE))
        return value

    def plus(first, second):
        if first is None:
            return second
        return first if second is None else first + second

    def scaled(scale, value):
        return None if value is None else scale * value

    residual = [one] + [None] * fields
    direction = [one] + [None] * (fields - 1)
    iterate = [None] * fields
    product_now = form(residual, direction)
    for step in range(fields):
        image = [None] * (fields + 1)
        for c in range(fields):
            if direction[c] is not None:
                image[c] = plus(image[c], SHIFT * direction[c])
                image[c + 1] = plus(image[c + 1], direction[c])
        alpha = product_now / form(image, direction)
        iterate = [plus(iterate[c], scaled(alpha, direction[c])) for c in range(fields)]
        residual = [plus(residual[a], scaled(-alpha, image[a])) for a in range(fields + 1)]
        if step + 1 < fields:
            product_next = form(residual, residual[:fields])
            beta = product_next / product_now
            direction = [plus(residual[c], scaled(beta, direction[c])) for c in range(fields)]
            product_now = product_next
    sound = checks[0]
    for check in checks[1:]:
        sound = sound & check
    return iterate, residual, sound


def decide_kernel(fields, width, mine_ref, theirs_ref, out_ref):
    _, _, sound = coefficients(mine_ref[...] + theirs_ref[...], fields, width)
    out_ref[...] = jnp.broadcast_to(jnp.where(sound, 1.0, 0.0), out_ref.shape)


def finish_kernel(fields, mine_ref, theirs_ref, *refs):
    value_refs = refs[: fields + 1]
    z_refs = refs[fields + 1 : 2 * fields + 1]
    solution_ref, residual_ref = refs[2 * fields + 1 :]
    shape = solution_ref.shape[1:]
    iterate, residual, _ = coefficients(mine_ref[...] + theirs_ref[...], fields, shape[1])
    answer = iterate[0] * z_refs[0][...]
    for c in range(1, fields):
        answer = answer + iterate[c] * z_refs[c][...]
    left_over = residual[0] * value_refs[0][...].reshape(shape)
    for a in range(1, fields + 1):
        left_over = left_over + residual[a] * value_refs[a][...]
    solution_ref[0] = answer
    residual_ref[0] = left_over


def step_by_step(bits, source, matrix, columns, senders, inverse, null_modes, groups_of, coarse_inv):
    highest = lax.Precision.HIGHEST
    row_count, width = source.shape
    turns, ghost_count = senders.shape
    extent = row_count + turns * ghost_count
    mode_count = null_modes.shape[1]
    group_count = coarse_inv.shape[0] // mode_count

    def table(size, index):
        return (jnp.arange(size, dtype=jnp.int32)[:, None] == index[None, :]).astype(f32)

    column_table = table(extent, columns.reshape(-1))
    sender_table = table(row_count, senders.reshape(-1))
    group_table = table(group_count, groups_of)

    def precondition(residual):
        local = jnp.einsum("rmb,rb->rm", null_modes, residual, precision=highest)
        total = lax.psum(jnp.dot(group_table, local, precision=highest), "coarse")
        solved = jnp.dot(coarse_inv, total.reshape(-1), precision=highest)
        per_row = jnp.dot(
            group_table.T, solved.reshape(group_count, mode_count), precision=highest
        )
        coarse = jnp.einsum("rmb,rm->rb", null_modes, per_row, precision=highest)
        return jnp.einsum("rab,rb->ra", inverse, residual, precision=highest) + coarse

    def operate(field):
        transposed = jnp.einsum("rkab,ra->rkb", matrix, field, precision=highest)
        spread = jnp.dot(column_table, transposed.reshape(-1, width), precision=highest)
        sent = jnp.dot(sender_table.T, field, precision=highest)
        rims = []
        returned = []
        for turn in range(turns):
            start = turn * ghost_count
            packet = jnp.concatenate(
                [
                    sent[start : start + ghost_count],
                    spread[row_count + start : row_count + start + ghost_count],
                ],
                axis=0,
            )
            arrived = partner(packet, "sub", bits[turn])
            rims.append(arrived[:ghost_count])
            returned.append(arrived[ghost_count:])
        extended = jnp.concatenate([field] + rims, axis=0)
        picked = jnp.dot(column_table.T, extended, precision=highest)
        picked = picked.reshape(row_count, -1, width)
        forward = jnp.einsum("rkab,rkb->ra", matrix, picked, precision=highest)
        back = jnp.dot(sender_table, jnp.concatenate(returned, axis=0), precision=highest)
        return 0.5 * (forward + (spread[:row_count] + back))

    def everywhere(first, second):
        return lax.psum(jnp.sum(first * second), ("sub", "coarse"))

    def body(step, state):
        answer, residual, direction, product_now = state
        precond = precondition(residual)
        product_next = everywhere(residual, precond)
        ratio = jnp.where(step == 0, 0.0, product_next / product_now)
        direction = precond + ratio * direction
        image = operate(direction)
        alpha = product_next / everywhere(direction, image)
        return (answer + alpha * direction, residual - alpha * image, direction, product_next)

    zeros = jnp.zeros_like(source)
    answer, residual, _, _ = lax.fori_loop(
        0, ITERS, body, (zeros, source, zeros, jnp.ones((), f32))
    )
    return answer[None], residual[None]


def on_device(
    right_side,
    blocks,
    pattern,
    send_rows,
    inverse_blocks,
    margin_blocks,
    near_null,
    aggregate,
    coarse_inverse,
):
    rows, width = right_side.shape[1:]
    slots = blocks.shape[2]
    turns, ghosts = send_rows.shape[1:]
    extent = rows + turns * ghosts
    modes = near_null.shape[2]
    levels = lax.axis_size("sub").bit_length() - 1
    bits = [turn * levels // turns for turn in range(turns)]
    flip = [(0, 1), (1, 0)]
    row_shape = (rows, width)
    packet = (2 * ghosts, width)
    parts = rows * slots
    ghost_total = turns * ghosts
    parts_scratch = [pltpu.VMEM((parts, width), f32)]
    spread_scratch = parts_scratch + [
        pltpu.VMEM((slots, extent, width), f32),
        pltpu.SMEM((2, 128), jnp.int32),
        pltpu.SemaphoreType.DMA,
    ]
    null_view = jnp.transpose(near_null, (0, 2, 1, 3))
    pattern_view = jnp.transpose(pattern, (2, 0, 1))

    def swap(array):
        return lax.ppermute(array, "coarse", flip)

    packs = call(
        pack_kernel,
        [(ghosts, width * width // 128, 128)] * turns,
        [VMEM] + [ANY] * REPEATS,
        [margin_blocks] * (1 + REPEATS),
        name="pack_margin",
    )
    gathered = [partner(packs[turn], "sub", bits[turn]) for turn in range(turns)]
    offset, wide_offset, mine = call(
        restrict_kernel,
        [((rows, 128), jnp.int32), ((parts, 128), jnp.int32), (1, 128)],
        [VMEM, VMEM, SMEM],
        [right_side, null_view, aggregate],
        name="restrict",
    )
    theirs = swap(mine)
    pick, send, back, index = call(
        table_kernel,
        [
            ((parts, 3 * extent), bf16),
            ((ghost_total, 3 * rows), bf16),
            ((rows, 3 * ghost_total), bf16),
            ((2, 128), jnp.int32),
        ],
        [SMEM, SMEM],
        [pattern_view, send_rows],
        scratch=[pltpu.VMEM((parts, 128), f32), pltpu.VMEM((ghost_total, 128), f32)],
        name="tables",
    )
    source, null_modes, solver = right_side, null_view, coarse_inverse
    (held,) = call(
        load_kernel,
        [blocks.shape],
        [ANY],
        [blocks],
        scratch=[pltpu.SemaphoreType.DMA] * 4,
        name="load_blocks",
        cost=8000000,
    )
    (row,) = call(
        local_row_kernel,
        [row_shape],
        [VMEM, VMEM],
        [right_side, inverse_blocks],
        name="local_rows",
    )
    base, wide = call(
        base_kernel,
        [row_shape, (width // (128 - width), ghost_total, 128)],
        [VMEM] * 8,
        [source, send, row, mine, theirs, solver, null_modes, offset],
        name="first_base",
    )
    half = modes // 2
    early_modes, late_modes = (
        call(
            functools.partial(modes_kernel, first),
            [(count, parts, width)],
            [VMEM, VMEM],
            [held, null_modes],
            name="spread_modes",
        )[0]
        for first, count in ((0, half), (half, modes - half))
    )
    base, early_modes = lax.optimization_barrier([base, early_modes])
    z, own, *packets = call(
        functools.partial(first_kernel, turns),
        [row_shape, row_shape] + [packet] * turns,
        [VMEM] * (turns + 5),
        [*gathered[::-1], base, wide, back, held, index],
        scratch=spread_scratch,
        name="first_spread",
    )
    (combined,) = call(
        functools.partial(combine_kernel, turns),
        [(rows, width, width)],
        [VMEM, SMEM] + [VMEM] * turns,
        [inverse_blocks, send_rows, *gathered],
        name="combine",
    )
    values = [source]
    fields = [z]
    for step in range(ITERS - 1):
        arrived = [partner(packets[turn], "sub", bits[turn]) for turn in range(turns)]
        if step == 0:
            combined, late_modes, *arrived = lax.optimization_barrier(
                [combined, late_modes, *arrived[::-1]]
            )
            arrived = arrived[::-1]
        following, mine = call(
            functools.partial(apply_kernel, turns),
            [row_shape, (1, 128)],
            [VMEM] * (turns + 8),
            [values[-1], fields[-1], own, *arrived[::-1], held, pick, back, null_modes, offset],
            scratch=parts_scratch,
            name="apply",
        )
        values.append(following)
        theirs = swap(mine)
        row, local = call(
            local_kernel,
            [row_shape, (parts, width)],
            [VMEM, VMEM, VMEM],
            [following, combined, held],
            name="local_inverse",
        )
        inputs = [local, row, mine, theirs, solver, null_modes, offset, wide_offset]
        inputs += [early_modes, late_modes, index]
        if step + 2 < ITERS:
            z, own, *packets = call(
                functools.partial(spread_kernel, turns),
                [row_shape, row_shape] + [packet] * turns,
                [VMEM] * 11,
                inputs,
                scratch=spread_scratch,
                name="spread",
            )
        else:
            (early,) = call(
                functools.partial(early_dots_kernel, ITERS),
                [(1, 128)],
                [VMEM] * (2 * ITERS - 1),
                [*values, *fields],
                name="early_dots",
            )
            z, own, payload = call(
                functools.partial(last_spread_kernel, ITERS),
                [row_shape, row_shape, (lax.axis_size("sub"), 2 * ghost_total, 128)],
                [VMEM] * (12 + ITERS),
                [*inputs, early, *values],
                scratch=spread_scratch[:2]
                + [pltpu.VMEM((2 * ghost_total, 128), f32)]
                + spread_scratch[2:],
                name="last_spread",
            )
        fields.append(z)
    lines = lax.all_to_all(payload, "sub", 0, 0)
    (mine,) = call(
        functools.partial(total_kernel, bits, ITERS, width),
        [(1, 128)],
        [VMEM],
        [lines],
        name="totals",
    )
    theirs = swap(mine)
    (following,) = call(
        functools.partial(last_kernel, bits),
        [row_shape],
        [VMEM] * 7,
        [values[-1], z, own, lines, held, pick, back],
        scratch=parts_scratch,
        name="last_apply",
    )
    values.append(following)
    (sound,) = call(
        functools.partial(decide_kernel, ITERS, width),
        [(1, 128)],
        [VMEM, VMEM],
        [mine, theirs],
        name="decide",
    )

    def finish():
        return tuple(
            call(
                functools.partial(finish_kernel, ITERS),
                [right_side.shape] * 2,
                [VMEM] * (2 * ITERS + 3),
                [mine, theirs, *values, *fields],
                name="finish",
            )
        )

    def again():
        nought = sound[0, 0]
        whole = nought.astype(jnp.int32)
        return step_by_step(
            bits,
            right_side[0] + nought,
            blocks[0] + nought,
            pattern[0] + whole,
            send_rows[0] + whole,
            combined + nought,
            near_null[0] + nought,
            aggregate[0] + whole,
            coarse_inverse[0] + nought,
        )

    return lax.cond(sound[0, 0] > 0.5, finish, again)


def solution(mesh):
    in_specs = (
        P("coarse", "sub", None),
        P("coarse", "sub", None, None, None),
        P("coarse", "sub", None),
        P("coarse", "sub", None),
        P("coarse", "sub", None, None),
        P("coarse", "sub", None, None),
        P("coarse", "sub", None, None),
        P("coarse", "sub"),
        P("sub", None, None),
    )
    out_specs = (P("coarse", "sub", None), P("coarse", "sub", None))
    return jax.shard_map(
        on_device, mesh=mesh, in_specs=in_specs, out_specs=out_specs, check_vma=False
    )
```

```python
import functools

import jax
import jax.numpy as jnp
from jax import lax
from jax.experimental import pallas as pl
from jax.experimental.pallas import tpu as pltpu
from jax.sharding import PartitionSpec as P

ITERS = 3
SHIFT = 2.0
REPEATS = 16
LIMIT = 200.0
LARGE = 1e30

f32 = jnp.float32
bf16 = jnp.bfloat16
VMEM = pl.BlockSpec(memory_space=pltpu.VMEM)
ANY = pl.BlockSpec(memory_space=pl.ANY)
SMEM = pl.BlockSpec(memory_space=pltpu.SMEM)


def partner(array, axis, bit):
    return lax.ppermute(array, axis, [(i, i ^ 1 << bit) for i in range(lax.axis_size(axis))])


def call(kernel, outs, in_specs, args, scratch=(), name=None, cost=100000):
    return pl.pallas_call(
        kernel,
        out_shape=[
            jax.ShapeDtypeStruct(*(out if isinstance(out[0], tuple) else (out, f32))) for out in outs
        ],
        in_specs=in_specs,
        out_specs=[VMEM] * len(outs),
        scratch_shapes=list(scratch),
        compiler_params=pltpu.CompilerParams(vmem_limit_bytes=12 * 1024 * 1024),
        cost_estimate=pl.CostEstimate(flops=0, bytes_accessed=cost, transcendentals=0),
        name=name,
    )(*args)


def eye_mask(width):
    return lax.broadcasted_iota(jnp.int32, (width, width), 0) == lax.broadcasted_iota(
        jnp.int32, (width, width), 1
    )


def to_column(row, eye):
    return jnp.sum(jnp.where(eye, row, 0.0), axis=1, keepdims=True)


def to_row(column, eye):
    return jnp.sum(jnp.where(eye, column, 0.0), axis=0, keepdims=True)


def restrict(null_ref, offset_ref, field):
    offset = offset_ref[...]
    total = jnp.zeros(offset.shape, f32)
    for mode in range(null_ref.shape[1]):
        dots = jnp.sum(null_ref[0, mode] * field, axis=1, keepdims=True)
        total = total + jnp.where(offset == mode, dots, 0.0)
    return jnp.sum(total, axis=0, keepdims=True)


def coarse_solve(mine_ref, theirs_ref, solver_ref):
    size = solver_ref.shape[1]
    total = mine_ref[...] + theirs_ref[...]
    solved = jnp.sum(solver_ref[0] * total[:, :size], axis=1, keepdims=True)
    return to_row(solved, eye_mask(size))


def coarse_combine(flat, offset, terms):
    offset = offset[:, : flat.shape[1]]
    field = None
    for mode, term in enumerate(terms):
        weight = jnp.sum(jnp.where(offset == mode, flat, 0.0), axis=1, keepdims=True)
        field = term * weight if field is None else field + term * weight
    return field


def coarse_field(mine_ref, theirs_ref, solver_ref, null_ref, offset_ref):
    flat = coarse_solve(mine_ref, theirs_ref, solver_ref)
    terms = [null_ref[0, mode] for mode in range(null_ref.shape[1])]
    return coarse_combine(flat, offset_ref[...], terms)


def thirds(value):
    high = value.astype(bf16)
    rest = value - high.astype(f32)
    middle = rest.astype(bf16)
    low = (rest - middle.astype(f32)).astype(bf16)
    return jnp.concatenate([high, middle, low], axis=0)


def select_rows(table_ref, value):
    return jnp.dot(table_ref[...], thirds(value), preferred_element_type=f32)


def triple(table):
    return jnp.concatenate([table.astype(bf16)] * 3, axis=1)


def pack_kernel(margin_ref, *refs):
    outs = refs[REPEATS:]
    turns = len(outs)
    ghosts, _, _ = outs[0].shape
    width = margin_ref.shape[2]
    tall = width * width // 128
    side = 128 - width
    rest = width - tall
    for turn in range(turns):
        for g in range(ghosts):
            block = margin_ref[0, turn * ghosts + g]
            outs[turn][g, :, 0:width] = block[:tall]
            for piece in range(width // side):
                outs[turn][g, piece * rest : (piece + 1) * rest, width:128] = block[
                    tall:, piece * side : (piece + 1) * side
                ]


def restrict_kernel(field_ref, null_ref, aggregate_ref, offset_ref, wide_offset_ref, mine_ref):
    modes = null_ref.shape[1]
    lane = lax.broadcasted_iota(jnp.int32, (1, 128), 1)
    for i in range(offset_ref.shape[0]):
        offset = lane - aggregate_ref[0, i] * modes
        offset_ref[i : i + 1, :] = offset
        each = wide_offset_ref.shape[0] // offset_ref.shape[0]
        wide_offset_ref[i * each : (i + 1) * each, :] = jnp.broadcast_to(offset, (each, 128))
    mine_ref[...] = restrict(null_ref, offset_ref, field_ref[0])


def table_kernel(
    pattern_ref, senders_ref, pick_ref, send_ref, back_ref, index_ref, table_ref, send_table_ref
):
    slots, _, rows = pattern_ref.shape
    turns, ghosts = senders_ref.shape[1:]
    extent = pick_ref.shape[1] // 3
    lane = lax.broadcasted_iota(jnp.int32, (1, 128), 1)
    columns = jnp.zeros((1, 128), jnp.int32)
    for i in range(rows):
        for j in range(slots):
            at = i * slots + j
            table_ref[at : at + 1, :] = jnp.where(lane == pattern_ref[j, 0, i], 1.0, 0.0)
            columns = jnp.where(lane == at, pattern_ref[j, 0, i], columns)
    index_ref[0:1, :] = columns
    sent = jnp.zeros((1, 128), jnp.int32)
    for turn in range(turns):
        for g in range(ghosts):
            at = turn * ghosts + g
            send_table_ref[at : at + 1, :] = jnp.where(lane == senders_ref[0, turn, g], 1.0, 0.0)
            sent = jnp.where(lane == at, senders_ref[0, turn, g], sent)
    index_ref[1:2, :] = sent
    table = table_ref[...]
    pick_ref[...] = triple(table[:, :extent])
    send_table = send_table_ref[...]
    send_ref[...] = triple(send_table[:, :rows])
    back_ref[...] = triple(send_table.T[:rows])


def load_kernel(source_ref, out_ref, *sems):
    quarter = source_ref.shape[1] // len(sems)
    copies = [
        pltpu.make_async_copy(
            source_ref.at[:, pl.ds(at * quarter, quarter)],
            out_ref.at[:, pl.ds(at * quarter, quarter)],
            sem,
        )
        for at, sem in enumerate(sems)
    ]
    for copy in copies:
        copy.start()
    for copy in copies:
        copy.wait()


def local_row_kernel(field_ref, inverse_ref, row_ref):
    rows, width = row_ref.shape
    eye = eye_mask(width)
    for i in range(rows):
        column = jnp.sum(inverse_ref[0, i] * field_ref[0, i : i + 1, :], axis=1, keepdims=True)
        row_ref[i : i + 1, :] = to_row(column, eye)


def local_kernel(field_ref, inverse_ref, blocks_ref, row_ref, parts_ref):
    rows, width = row_ref.shape
    eye = eye_mask(width)
    for i in range(rows):
        column = jnp.sum(inverse_ref[i] * field_ref[i : i + 1, :], axis=1, keepdims=True)
        row_ref[i : i + 1, :] = to_row(column, eye)
        spread_block_row(blocks_ref, parts_ref, i, column)


def modes_kernel(first, blocks_ref, null_ref, out_ref):
    rows, width = null_ref.shape[2:]
    modes = out_ref.shape[0]
    slots = blocks_ref.shape[2]
    eye = eye_mask(width)

    def body(i, carry):
        columns = [
            to_column(null_ref[0, first + mode, pl.ds(i, 1), :], eye) for mode in range(modes)
        ]
        for j in range(slots):
            sums = [None] * modes
            for start in range(0, width, 8):
                tile = blocks_ref[0, i, j, start : start + 8, :]
                for mode in range(modes):
                    term = tile * columns[mode][start : start + 8]
                    sums[mode] = term if start == 0 else sums[mode] + term
            for mode in range(modes):
                out_ref[mode, pl.ds(i * slots + j, 1), :] = jnp.sum(
                    sums[mode], axis=0, keepdims=True
                )
        return carry

    lax.fori_loop(0, rows, body, 0, unroll=True)


def spread_block_row(blocks_ref, parts_ref, i, column):
    slots, width = blocks_ref.shape[2:4]
    for j in range(slots):
        part = blocks_ref[0, i, j, 0:8, :] * column[0:8]
        for start in range(8, width, 8):
            part = part + blocks_ref[0, i, j, start : start + 8, :] * column[start : start + 8]
        at = i * slots + j
        parts_ref[at : at + 1, :] = jnp.sum(part, axis=0, keepdims=True)


def scatter_rows(parts_ref, slots_ref, indices_ref, rows):
    slots = slots_ref.shape[0]
    for i in range(rows):
        slots_ref[0, i : i + 1, :] = parts_ref[i * slots : i * slots + 1, :]
        for j in range(1, slots):
            at = i * slots + j
            slots_ref[j, pl.ds(indices_ref[0, at], 1), :] = parts_ref[at : at + 1, :]
    spread = slots_ref[0]
    for j in range(1, slots):
        spread = spread + slots_ref[j]
    return spread


def finish_spread(parts_ref, slots_ref, indices_ref, z_ref, own_ref, packets):
    turns = len(packets)
    rows = z_ref.shape[0]
    ghosts = packets[0].shape[0] // 2
    spread = scatter_rows(parts_ref, slots_ref, indices_ref, rows)
    own_ref[...] = spread[:rows]
    for turn in range(turns):
        for g in range(ghosts):
            at = indices_ref[1, turn * ghosts + g]
            packets[turn][g : g + 1, :] = z_ref[pl.ds(at, 1), :]
        start = rows + turn * ghosts
        packets[turn][ghosts:, :] = spread[start : start + ghosts]


def margin_row(packed_ref, g, wide_ref, at, eye, inside):
    pieces = wide_ref.shape[0]
    tall = packed_ref.shape[1]
    rest = tall // pieces
    products = [
        packed_ref[g, piece * rest : (piece + 1) * rest, :] * wide_ref[piece, at : at + 1, :]
        for piece in range(pieces)
    ]
    beside = products[0]
    for product in products[1:]:
        beside = beside + product
    main = [jnp.where(inside, product, 0.0) for product in products]
    columns = [jnp.sum(part, axis=1, keepdims=True) for part in main]
    columns.append(jnp.sum(jnp.where(inside, 0.0, beside), axis=1, keepdims=True))
    row = None
    for piece, column in enumerate(columns):
        part = jnp.where(eye[piece * rest : (piece + 1) * rest], column, 0.0)
        row = part if row is None else row + part
    return jnp.sum(row, axis=0, keepdims=True)


def margin_rows(packed, wide_ref, eye):
    ghosts = packed[0].shape[0]
    width = eye.shape[0]
    inside = lax.broadcasted_iota(jnp.int32, (1, 128), 1) < width
    out = []
    for turn, ref in enumerate(packed):
        for g in range(ghosts):
            out.append(margin_row(ref, g, wide_ref, turn * ghosts + g, eye, inside))
    return jnp.concatenate(out, axis=0)


def base_kernel(
    field_ref,
    send_ref,
    row_ref,
    mine_ref,
    theirs_ref,
    solver_ref,
    null_ref,
    offset_ref,
    base_ref,
    wide_ref,
):
    picked = select_rows(send_ref, field_ref[0])
    width = picked.shape[1]
    side = 128 - width
    for piece in range(wide_ref.shape[0]):
        wide_ref[piece, :, :width] = picked
        wide_ref[piece, :, width:] = picked[:, piece * side : (piece + 1) * side]
    coarse = coarse_field(mine_ref, theirs_ref, solver_ref, null_ref, offset_ref)
    base_ref[...] = row_ref[...] + coarse


def combine_kernel(turns, inverse_ref, senders_ref, *refs):
    gathered = refs[:turns]
    (combined_ref,) = refs[turns:]
    ghosts, tall = gathered[0].shape[:2]
    width = inverse_ref.shape[2]
    side = 128 - width
    rest = width - tall
    combined_ref[...] = inverse_ref[0]
    for turn in range(turns):
        for g in range(ghosts):
            at = senders_ref[0, turn, g]
            combined_ref[at, 0:tall, :] += gathered[turn][g, :, 0:width]
            for piece in range(width // side):
                combined_ref[at, tall:, piece * side : (piece + 1) * side] += gathered[turn][
                    g, piece * rest : (piece + 1) * rest, width:128
                ]


def first_kernel(turns, *refs):
    packed = refs[:turns][::-1]
    base_ref, wide_ref, back_ref, blocks_ref, index_ref, z_ref, own_ref = refs[turns : turns + 7]
    packets = refs[turns + 7 : 2 * turns + 7]
    parts_ref, slots_ref, indices_ref, sem = refs[2 * turns + 7 :]
    fetch = pltpu.make_async_copy(index_ref, indices_ref, sem)
    fetch.start()
    slots_ref[...] = jnp.zeros(slots_ref.shape, f32)
    rows, width = z_ref.shape
    eye = eye_mask(width)
    margin = margin_rows(packed, wide_ref, eye)
    z = base_ref[...] + select_rows(back_ref, margin)
    z_ref[...] = z
    for i in range(rows):
        spread_block_row(blocks_ref, parts_ref, i, to_column(z[i : i + 1], eye))
    fetch.wait()
    finish_spread(parts_ref, slots_ref, indices_ref, z_ref, own_ref, packets)


def spread_rows(
    local_ref,
    row_ref,
    mine_ref,
    theirs_ref,
    solver_ref,
    null_ref,
    offset_ref,
    wide_offset_ref,
    early_modes_ref,
    late_modes_ref,
    z_ref,
    parts_ref,
):
    flat = coarse_solve(mine_ref, theirs_ref, solver_ref)
    modes = null_ref.shape[1]
    terms = [ref[mode] for ref in (early_modes_ref, late_modes_ref) for mode in range(ref.shape[0])]
    added = coarse_combine(flat, wide_offset_ref[...], terms)
    parts_ref[...] = local_ref[...] + added
    coarse = coarse_combine(flat, offset_ref[...], [null_ref[0, mode] for mode in range(modes)])
    z_ref[...] = row_ref[...] + coarse


def spread_kernel(turns, *refs):
    index_ref, z_ref, own_ref = refs[10:13]
    packets = refs[13 : 13 + turns]
    parts_ref, slots_ref, indices_ref, sem = refs[13 + turns :]
    fetch = pltpu.make_async_copy(index_ref, indices_ref, sem)
    fetch.start()
    slots_ref[...] = jnp.zeros(slots_ref.shape, f32)
    spread_rows(*refs[:10], z_ref, parts_ref)
    fetch.wait()
    finish_spread(parts_ref, slots_ref, indices_ref, z_ref, own_ref, packets)


def dot_at(lane, at, first, second, packed):
    dot = jnp.sum(jnp.sum(first * second, axis=0, keepdims=True), axis=1, keepdims=True)
    return jnp.where(lane == at, dot, packed)


def early_dots_kernel(fields, *refs):
    value_refs = refs[:fields]
    z_refs = refs[fields:-1]
    rows, width = z_refs[0].shape
    lane = lax.broadcasted_iota(jnp.int32, (1, 128), 1)
    packed = jnp.zeros((1, 128), f32)
    for a in range(fields):
        value = value_refs[a][...].reshape(rows, width)
        for c, z_at in enumerate(z_refs):
            packed = dot_at(lane, width + a * fields + c, value, z_at[...], packed)
    refs[-1][...] = packed


def last_spread_kernel(fields, *refs):
    index_ref, early_ref = refs[10:12]
    value_refs = refs[12 : 12 + fields]
    z_ref, own_ref, payload_ref, parts_ref, slots_ref, line_ref, indices_ref, sem = refs[12 + fields :]
    fetch = pltpu.make_async_copy(index_ref, indices_ref, sem)
    fetch.start()
    slots_ref[...] = jnp.zeros(slots_ref.shape, f32)
    line_ref[...] = jnp.zeros(line_ref.shape, f32)
    spread_rows(*refs[:10], z_ref, parts_ref)
    rows, width = z_ref.shape
    ghosts = line_ref.shape[0] // 2
    z = z_ref[...]
    lane = lax.broadcasted_iota(jnp.int32, (1, 128), 1)
    packed = early_ref[...]
    for a in range(fields):
        value = value_refs[a][...].reshape(rows, width)
        packed = dot_at(lane, width + a * fields + fields - 1, value, z, packed)
    fetch.wait()
    spread = scatter_rows(parts_ref, slots_ref, indices_ref, rows)
    own = spread[:rows]
    own_ref[...] = own
    packed = dot_at(lane, width + fields * fields, z, own, packed)
    line_ref[0:1, :] = packed
    line_ref[0:ghosts, :width] = spread[rows:]
    for at in range(ghosts):
        line_ref[ghosts + at : ghosts + at + 1, :width] = z_ref[pl.ds(indices_ref[1, at], 1), :]
    line = line_ref[...]
    for device in range(payload_ref.shape[0]):
        payload_ref[device] = line


def total_kernel(bits, fields, width, lines_ref, out_ref):
    devices, height = lines_ref.shape[:2]
    ghosts = height // 2
    each = ghosts // len(bits)
    lane = lax.broadcasted_iota(jnp.int32, (1, 128), 1)
    packed = lines_ref[0, 0:1, :]
    for device in range(1, devices):
        packed = packed + lines_ref[device, 0:1, :]
    crossed = jnp.zeros((each, 128), f32)
    for device in range(devices):
        for turn, bit in enumerate(bits):
            start = turn * each
            crossed = crossed + (
                lines_ref[device, start : start + each, :]
                * lines_ref[device ^ (1 << bit), ghosts + start : ghosts + start + each, :]
            )
    crossed = jnp.where(lane < width, jnp.sum(crossed, axis=0, keepdims=True), 0.0)
    crossed = jnp.sum(crossed, axis=1, keepdims=True)
    at = lane == width + fields * fields
    out_ref[...] = packed + jnp.where(at, crossed, 0.0)


def apply_rows(rims, returned, z, own_ref, blocks_ref, pick_ref, back_ref, picked_ref):
    rows, width = z.shape
    slots = blocks_ref.shape[2]
    eye = eye_mask(width)
    extended = jnp.concatenate([z] + rims, axis=0)
    picked_ref[...] = select_rows(pick_ref, extended)
    returned = jnp.concatenate(returned, axis=0)
    back = own_ref[...] + select_rows(back_ref, returned)
    image = []
    for i in range(rows):
        total = None
        for j in range(slots):
            at = i * slots + j
            term = blocks_ref[0, i, j] * picked_ref[at : at + 1, :]
            total = term if total is None else total + term
        column = jnp.sum(total, axis=1, keepdims=True)
        image.append(to_row(column, eye))
    return 0.5 * (jnp.concatenate(image, axis=0) + back)


def apply_kernel(turns, field_ref, z_ref, own_ref, *refs):
    arrived = refs[:turns][::-1]
    (
        blocks_ref,
        pick_ref,
        back_ref,
        null_ref,
        offset_ref,
        next_ref,
        coarse_ref,
        picked_ref,
    ) = refs[turns:]
    ghosts = arrived[0].shape[0] // 2
    rims = [ref[0:ghosts, :] for ref in arrived]
    returned = [ref[ghosts:, :] for ref in arrived]
    image = apply_rows(
        rims, returned, z_ref[...], own_ref, blocks_ref, pick_ref, back_ref, picked_ref
    )
    following = image - SHIFT * field_ref[...].reshape(image.shape)
    next_ref[...] = following
    coarse_ref[...] = restrict(null_ref, offset_ref, following)


def last_kernel(
    bits,
    field_ref,
    z_ref,
    own_ref,
    lines_ref,
    blocks_ref,
    pick_ref,
    back_ref,
    next_ref,
    picked_ref,
):
    width = z_ref.shape[1]
    ghosts = lines_ref.shape[1] // 2
    each = ghosts // len(bits)
    here = lax.axis_index("sub")
    rims = []
    returned = []
    for turn, bit in enumerate(bits):
        start = turn * each
        there = jnp.bitwise_xor(here, 1 << bit)
        returned.append(lines_ref[there, start : start + each, :width])
        rims.append(lines_ref[there, ghosts + start : ghosts + start + each, :width])
    image = apply_rows(
        rims, returned, z_ref[...], own_ref, blocks_ref, pick_ref, back_ref, picked_ref
    )
    next_ref[...] = image - SHIFT * field_ref[...]


def coefficients(total, fields, width):
    lane = lax.broadcasted_iota(jnp.int32, (1, 128), 1)

    def product(at):
        return jnp.sum(jnp.where(lane == width + at, total, 0.0), axis=1, keepdims=True)

    gram = [[product(a * fields + c) for c in range(fields)] for a in range(fields)]
    last = fields - 1
    final = [gram[c + 1][last] + SHIFT * gram[c][last] for c in range(last)]
    final.append(product(fields * fields))
    gram.append([final[c] - SHIFT * gram[last][c] for c in range(fields)])
    one = jnp.ones((1, 1), f32)
    checks = []

    def form(left, right):
        value = jnp.zeros((1, 1), f32)
        size = jnp.zeros((1, 1), f32)
        for a, left_at in enumerate(left):
            if left_at is None:
                continue
            for c, right_at in enumerate(right):
                if right_at is not None:
                    term = left_at * right_at * gram[a][c]
                    value = value + term
                    size = size + jnp.abs(term)
        checks.append((size <= LIMIT * jnp.abs(value)) & (size < LARGE) & (size > 1.0 / LARGE))
        return value

    def plus(first, second):
        if first is None:
            return second
        return first if second is None else first + second

    def scaled(scale, value):
        return None if value is None else scale * value

    residual = [one] + [None] * fields
    direction = [one] + [None] * (fields - 1)
    iterate = [None] * fields
    product_now = form(residual, direction)
    for step in range(fields):
        image = [None] * (fields + 1)
        for c in range(fields):
            if direction[c] is not None:
                image[c] = plus(image[c], SHIFT * direction[c])
                image[c + 1] = plus(image[c + 1], direction[c])
        alpha = product_now / form(image, direction)
        iterate = [plus(iterate[c], scaled(alpha, direction[c])) for c in range(fields)]
        residual = [plus(residual[a], scaled(-alpha, image[a])) for a in range(fields + 1)]
        if step + 1 < fields:
            product_next = form(residual, residual[:fields])
            beta = product_next / product_now
            direction = [plus(residual[c], scaled(beta, direction[c])) for c in range(fields)]
            product_now = product_next
    sound = checks[0]
    for check in checks[1:]:
        sound = sound & check
    return iterate, residual, sound


def decide_kernel(fields, width, mine_ref, theirs_ref, out_ref):
    _, _, sound = coefficients(mine_ref[...] + theirs_ref[...], fields, width)
    out_ref[...] = jnp.broadcast_to(jnp.where(sound, 1.0, 0.0), out_ref.shape)


def finish_kernel(fields, mine_ref, theirs_ref, *refs):
    value_refs = refs[: fields + 1]
    z_refs = refs[fields + 1 : 2 * fields + 1]
    solution_ref, residual_ref = refs[2 * fields + 1 :]
    shape = solution_ref.shape[1:]
    iterate, residual, _ = coefficients(mine_ref[...] + theirs_ref[...], fields, shape[1])
    answer = iterate[0] * z_refs[0][...]
    for c in range(1, fields):
        answer = answer + iterate[c] * z_refs[c][...]
    left_over = residual[0] * value_refs[0][...].reshape(shape)
    for a in range(1, fields + 1):
        left_over = left_over + residual[a] * value_refs[a][...]
    solution_ref[0] = answer
    residual_ref[0] = left_over


def step_by_step(bits, source, matrix, columns, senders, inverse, null_modes, groups_of, coarse_inv):
    highest = lax.Precision.HIGHEST
    row_count, width = source.shape
    turns, ghost_count = senders.shape
    extent = row_count + turns * ghost_count
    mode_count = null_modes.shape[1]
    group_count = coarse_inv.shape[0] // mode_count

    def table(size, index):
        return (jnp.arange(size, dtype=jnp.int32)[:, None] == index[None, :]).astype(f32)

    column_table = table(extent, columns.reshape(-1))
    sender_table = table(row_count, senders.reshape(-1))
    group_table = table(group_count, groups_of)

    def precondition(residual):
        local = jnp.einsum("rmb,rb->rm", null_modes, residual, precision=highest)
        total = lax.psum(jnp.dot(group_table, local, precision=highest), "coarse")
        solved = jnp.dot(coarse_inv, total.reshape(-1), precision=highest)
        per_row = jnp.dot(
            group_table.T, solved.reshape(group_count, mode_count), precision=highest
        )
        coarse = jnp.einsum("rmb,rm->rb", null_modes, per_row, precision=highest)
        return jnp.einsum("rab,rb->ra", inverse, residual, precision=highest) + coarse

    def operate(field):
        transposed = jnp.einsum("rkab,ra->rkb", matrix, field, precision=highest)
        spread = jnp.dot(column_table, transposed.reshape(-1, width), precision=highest)
        sent = jnp.dot(sender_table.T, field, precision=highest)
        rims = []
        returned = []
        for turn in range(turns):
            start = turn * ghost_count
            packet = jnp.concatenate(
                [
                    sent[start : start + ghost_count],
                    spread[row_count + start : row_count + start + ghost_count],
                ],
                axis=0,
            )
            arrived = partner(packet, "sub", bits[turn])
            rims.append(arrived[:ghost_count])
            returned.append(arrived[ghost_count:])
        extended = jnp.concatenate([field] + rims, axis=0)
        picked = jnp.dot(column_table.T, extended, precision=highest)
        picked = picked.reshape(row_count, -1, width)
        forward = jnp.einsum("rkab,rkb->ra", matrix, picked, precision=highest)
        back = jnp.dot(sender_table, jnp.concatenate(returned, axis=0), precision=highest)
        return 0.5 * (forward + (spread[:row_count] + back))

    def everywhere(first, second):
        return lax.psum(jnp.sum(first * second), ("sub", "coarse"))

    def body(step, state):
        answer, residual, direction, product_now = state
        precond = precondition(residual)
        product_next = everywhere(residual, precond)
        ratio = jnp.where(step == 0, 0.0, product_next / product_now)
        direction = precond + ratio * direction
        image = operate(direction)
        alpha = product_next / everywhere(direction, image)
        return (answer + alpha * direction, residual - alpha * image, direction, product_next)

    zeros = jnp.zeros_like(source)
    answer, residual, _, _ = lax.fori_loop(
        0, ITERS, body, (zeros, source, zeros, jnp.ones((), f32))
    )
    return answer[None], residual[None]


def on_device(
    right_side,
    blocks,
    pattern,
    send_rows,
    inverse_blocks,
    margin_blocks,
    near_null,
    aggregate,
    coarse_inverse,
):
    rows, width = right_side.shape[1:]
    slots = blocks.shape[2]
    turns, ghosts = send_rows.shape[1:]
    extent = rows + turns * ghosts
    modes = near_null.shape[2]
    levels = lax.axis_size("sub").bit_length() - 1
    bits = [turn * levels // turns for turn in range(turns)]
    flip = [(0, 1), (1, 0)]
    row_shape = (rows, width)
    packet = (2 * ghosts, width)
    parts = rows * slots
    ghost_total = turns * ghosts
    parts_scratch = [pltpu.VMEM((parts, width), f32)]
    spread_scratch = parts_scratch + [
        pltpu.VMEM((slots, extent, width), f32),
        pltpu.SMEM((2, 128), jnp.int32),
        pltpu.SemaphoreType.DMA,
    ]
    null_view = jnp.transpose(near_null, (0, 2, 1, 3))
    pattern_view = jnp.transpose(pattern, (2, 0, 1))

    def swap(array):
        return lax.ppermute(array, "coarse", flip)

    packs = call(
        pack_kernel,
        [(ghosts, width * width // 128, 128)] * turns,
        [VMEM] + [ANY] * REPEATS,
        [margin_blocks] * (1 + REPEATS),
        name="pack_margin",
    )
    gathered = [partner(packs[turn], "sub", bits[turn]) for turn in range(turns)]
    offset, wide_offset, mine = call(
        restrict_kernel,
        [((rows, 128), jnp.int32), ((parts, 128), jnp.int32), (1, 128)],
        [VMEM, VMEM, SMEM],
        [right_side, null_view, aggregate],
        name="restrict",
    )
    theirs = swap(mine)
    pick, send, back, index = call(
        table_kernel,
        [
            ((parts, 3 * extent), bf16),
            ((ghost_total, 3 * rows), bf16),
            ((rows, 3 * ghost_total), bf16),
            ((2, 128), jnp.int32),
        ],
        [SMEM, SMEM],
        [pattern_view, send_rows],
        scratch=[pltpu.VMEM((parts, 128), f32), pltpu.VMEM((ghost_total, 128), f32)],
        name="tables",
    )
    source, null_modes, solver = right_side, null_view, coarse_inverse
    (held,) = call(
        load_kernel,
        [blocks.shape],
        [ANY],
        [blocks],
        scratch=[pltpu.SemaphoreType.DMA] * 4,
        name="load_blocks",
        cost=8000000,
    )
    (row,) = call(
        local_row_kernel,
        [row_shape],
        [VMEM, VMEM],
        [right_side, inverse_blocks],
        name="local_rows",
    )
    base, wide = call(
        base_kernel,
        [row_shape, (width // (128 - width), ghost_total, 128)],
        [VMEM] * 8,
        [source, send, row, mine, theirs, solver, null_modes, offset],
        name="first_base",
    )
    half = modes // 2
    early_modes, late_modes = (
        call(
            functools.partial(modes_kernel, first),
            [(count, parts, width)],
            [VMEM, VMEM],
            [held, null_modes],
            name="spread_modes",
        )[0]
        for first, count in ((0, half), (half, modes - half))
    )
    base, early_modes = lax.optimization_barrier([base, early_modes])
    z, own, *packets = call(
        functools.partial(first_kernel, turns),
        [row_shape, row_shape] + [packet] * turns,
        [VMEM] * (turns + 5),
        [*gathered[::-1], base, wide, back, held, index],
        scratch=spread_scratch,
        name="first_spread",
    )
    (combined,) = call(
        functools.partial(combine_kernel, turns),
        [(rows, width, width)],
        [VMEM, SMEM] + [VMEM] * turns,
        [inverse_blocks, send_rows, *gathered],
        name="combine",
    )
    values = [source]
    fields = [z]
    for step in range(ITERS - 1):
        arrived = [partner(packets[turn], "sub", bits[turn]) for turn in range(turns)]
        if step == 0:
            combined, late_modes, *arrived = lax.optimization_barrier(
                [combined, late_modes, *arrived[::-1]]
            )
            arrived = arrived[::-1]
        following, mine = call(
            functools.partial(apply_kernel, turns),
            [row_shape, (1, 128)],
            [VMEM] * (turns + 8),
            [values[-1], fields[-1], own, *arrived[::-1], held, pick, back, null_modes, offset],
            scratch=parts_scratch,
            name="apply",
        )
        values.append(following)
        theirs = swap(mine)
        row, local = call(
            local_kernel,
            [row_shape, (parts, width)],
            [VMEM, VMEM, VMEM],
            [following, combined, held],
            name="local_inverse",
        )
        inputs = [local, row, mine, theirs, solver, null_modes, offset, wide_offset]
        inputs += [early_modes, late_modes, index]
        if step + 2 < ITERS:
            z, own, *packets = call(
                functools.partial(spread_kernel, turns),
                [row_shape, row_shape] + [packet] * turns,
                [VMEM] * 11,
                inputs,
                scratch=spread_scratch,
                name="spread",
            )
        else:
            (early,) = call(
                functools.partial(early_dots_kernel, ITERS),
                [(1, 128)],
                [VMEM] * (2 * ITERS - 1),
                [*values, *fields],
                name="early_dots",
            )
            z, own, payload = call(
                functools.partial(last_spread_kernel, ITERS),
                [row_shape, row_shape, (lax.axis_size("sub"), 2 * ghost_total, 128)],
                [VMEM] * (12 + ITERS),
                [*inputs, early, *values],
                scratch=spread_scratch[:2]
                + [pltpu.VMEM((2 * ghost_total, 128), f32)]
                + spread_scratch[2:],
                name="last_spread",
            )
        fields.append(z)
    lines = lax.all_to_all(payload, "sub", 0, 0)
    (mine,) = call(
        functools.partial(total_kernel, bits, ITERS, width),
        [(1, 128)],
        [VMEM],
        [lines],
        name="totals",
    )
    theirs = swap(mine)
    (following,) = call(
        functools.partial(last_kernel, bits),
        [row_shape],
        [VMEM] * 7,
        [values[-1], z, own, lines, held, pick, back],
        scratch=parts_scratch,
        name="last_apply",
    )
    values.append(following)
    (sound,) = call(
        functools.partial(decide_kernel, ITERS, width),
        [(1, 128)],
        [VMEM, VMEM],
        [mine, theirs],
        name="decide",
    )

    def finish():
        return tuple(
            call(
                functools.partial(finish_kernel, ITERS),
                [right_side.shape] * 2,
                [VMEM] * (2 * ITERS + 3),
                [mine, theirs, *values, *fields],
                name="finish",
            )
        )

    def again():
        nought = sound[0, 0]
        whole = nought.astype(jnp.int32)
        return step_by_step(
            bits,
            right_side[0] + nought,
            blocks[0] + nought,
            pattern[0] + whole,
            send_rows[0] + whole,
            combined + nought,
            near_null[0] + nought,
            aggregate[0] + whole,
            coarse_inverse[0] + nought,
        )

    return lax.cond(sound[0, 0] > 0.5, finish, again)


def solution(mesh):
    in_specs = (
        P("coarse", "sub", None),
        P("coarse", "sub", None, None, None),
        P("coarse", "sub", None),
        P("coarse", "sub", None),
        P("coarse", "sub", None, None),
        P("coarse", "sub", None, None),
        P("coarse", "sub", None, None),
        P("coarse", "sub"),
        P("sub", None, None),
    )
    out_specs = (P("coarse", "sub", None), P("coarse", "sub", None))
    return jax.shard_map(
        on_device, mesh=mesh, in_specs=in_specs, out_specs=out_specs, check_vma=False
    )
```
